32 devices in a mesh: dom: 2 (over y), frame: 4 (over z), query: 2 (over x), split: 2 (over core).
Axes of the slice: x: 2, y: 2, z: 4, core: 2. Of those that a mesh axis runs over, the one named last changes fastest.
Arguments:
- frames: bfloat16 [16, 1024, 256], P(('dom', 'frame')), parts along dimension 0, may hold values from -64 to 64
- query_frame: int32 [2048], P(('dom', 'query')), parts along dimension 0, may hold values from 0 to 7, as said below
- query_pixel: int32 [2, 2048], P(None, ('dom', 'query')), parts along dimension 1, may hold values from 0 to 31
- in_weight: bfloat16 [512, 512], replicated, may hold values from -0.25 to 0.25
- conv_weight: float32 [1, 3, 512], replicated, may hold values from -3 to 3
- up_weight: bfloat16 [1, 512, 2048], P(None, None, 'split'), may hold values from -0.25 to 0.25
- down_weight: bfloat16 [1, 2048, 512], P(None, 'split'), may hold values from -0.125 to 0.125
Outputs:
- tokens: bfloat16 [2048, 8, 512], P(('dom', 'query'), 'frame'), parts along dimension 0
The draws below stay inside these ranges and needn't reach their ends.
There are 2 independent parts, one for each index of `dom`. The reference program is written for one: setup_inputs(seed, part) draws one part's arguments, and reference() takes and returns one part's arrays. A program takes and returns all parts, laid end to end along the dimension named above; an argument that names none is the same for every part. Nothing has to cross between parts.
Inputs may be any that keep to these rules, and one draw needn't show every extreme that they name: `query_frame`: within each aligned group of 512 query points (one index of query), at most 384 start frames lie among any aligned 2 frames (one index of frame), and in every group some such frames hold exactly 384.
All inputs are finite; a program needn't handle non-finite values.
Results may differ from the reference program's by a relative error of at most 0.006.
Values may be sent and summed in bfloat16 or wider, within the bound.
No kernel may reach another device: no remote copies, remote signals or barrier semaphores. Data moves between devices by JAX's collectives and lax.ppermute only.
A program may use at most 64 MiB of HBM per device.

```python
import math
import jax
import jax.numpy as jnp
from jax import lax

C = 256
D = 512
FF = 2048
SIDE = 32
FR_DEV = 2
Q_DEV = 512
BLOCKS = 1
PIX = 1024
FRAMES = 8
QUERIES = 1024
CAP = 384


def draw_frames(key, part):
    first_key = jax.random.fold_in(key, 0)
    noise = jax.random.normal(first_key, (FRAMES, PIX, C), jnp.float32)
    values = noise
    return jnp.clip(values, -64.0, 64.0).astype(jnp.bfloat16)


def draw_query_frame(key, part):
    owners = FRAMES // FR_DEV
    groups = QUERIES // Q_DEV

    def one_group(group_key):
        hot_key, slot_key, frame_key, order_key = jax.random.split(group_key, 4)
        hot_owner = jax.random.randint(hot_key, (), 0, owners).astype(jnp.int32)
        slots = jax.random.permutation(slot_key, (owners - 1) * CAP)[:Q_DEV - CAP].astype(jnp.int32)
        rest_owner = slots // CAP
        rest_owner = rest_owner + (rest_owner >= hot_owner).astype(jnp.int32)
        owner = jnp.concatenate([jnp.full((CAP,), hot_owner, jnp.int32), rest_owner])
        chosen = owner * FR_DEV + jax.random.randint(frame_key, (Q_DEV,), 0, FR_DEV).astype(jnp.int32)
        shuffled = jax.random.permutation(order_key, Q_DEV)
        return chosen[shuffled]
    return jax.vmap(one_group)(jax.random.split(key, groups)).reshape(-1).astype(jnp.int32)


def set_ends(values, key, smallest, top_value):
    longest = values.shape.index(max(values.shape))
    spots = []
    for shift in (0, 1):
        where = [jax.random.randint(jax.random.fold_in(key, axis), (), 0, length) for axis, length in enumerate(values.shape)]
        where[longest] = (where[longest] + shift) % values.shape[longest]
        spots.append(tuple(where))
    return values.at[spots[0]].set(smallest).at[spots[1]].set(top_value)


def shard_levels(own_key, dims, cuts, smallest, top_value):
    loudness, own = 1.0, jax.random.fold_in(own_key, 6)
    for axis_at, shards_of in cuts:
        heights = jnp.exp(jax.random.uniform(jax.random.fold_in(own, axis_at), (shards_of,), jnp.float32, smallest / len(cuts), top_value / len(cuts)))
        loudness = loudness * jnp.repeat(heights, dims[axis_at] // shards_of).reshape([-1 if axis == axis_at else 1 for axis in range(len(dims))])
    return loudness


def gaussian(own_key, dims, spread, most, cuts=(), held_as=jnp.bfloat16):
    factor_of = shard_levels(own_key, dims, cuts, -0.22, 0.18) if cuts else 1.0
    drawn = jax.random.normal(own_key, dims, jnp.float32) * spread * factor_of
    return jnp.minimum(jnp.maximum(drawn, -most), most).astype(held_as)


def setup_inputs(seed: int = 0, part: int = 0) -> dict:
    arg_keys = jax.random.split(jax.random.key(seed), 8)
    part_splits = jax.random.split(jax.random.fold_in(arg_keys[7], part), 8)
    frames = draw_frames(jax.random.fold_in(jax.random.fold_in(arg_keys[7], part), 71), part)
    query_frame = draw_query_frame(jax.random.fold_in(jax.random.fold_in(arg_keys[7], part), 71), part)
    query_pixel = set_ends(jax.random.randint(part_splits[2], (2, QUERIES), 0, SIDE), jax.random.fold_in(part_splits[2], 1), 0, SIDE - 1).astype(jnp.int32)
    in_weight = gaussian(arg_keys[3], (2 * C, D), (2 * C) ** -0.5, 0.25)
    conv_weight = gaussian(arg_keys[4], (BLOCKS, 3, D), 0.5, 3.0, (), jnp.float32)
    up_weight = gaussian(arg_keys[5], (BLOCKS, D, FF), D ** -0.5, 0.25, ((2, 2),))
    down_weight = gaussian(arg_keys[6], (BLOCKS, FF, D), FF ** -0.5, 0.125, ((1, 2),))
    return dict(frames=frames, query_frame=query_frame, query_pixel=query_pixel, in_weight=in_weight, conv_weight=conv_weight, up_weight=up_weight, down_weight=down_weight)


def rms_scale(values, epsilon):
    return values / jnp.sqrt(lax.optimization_barrier(jnp.mean(values * values, axis=-1, keepdims=True)) + epsilon)

def reference(frames, query_frame, query_pixel, in_weight, conv_weight, up_weight, down_weight):
    pixel_index = (query_pixel[0] * SIDE + query_pixel[1]).astype(jnp.int32)
    query_features = frames[query_frame.astype(jnp.int32), pixel_index]
    factor = 1.0 / math.sqrt(C)

    def one_frame(feature_map):
        scores = jnp.dot(query_features, feature_map.T, preferred_element_type=jnp.float32) * factor
        peak = lax.optimization_barrier(jnp.max(scores, axis=-1, keepdims=True))
        expd = jnp.exp(scores - peak)
        weights = (expd / lax.optimization_barrier(jnp.sum(expd, axis=-1, keepdims=True))).astype(jnp.bfloat16)
        pooled = jnp.dot(weights, feature_map, preferred_element_type=jnp.float32)
        return rms_scale(pooled, 1e-06).astype(jnp.bfloat16)
    normed = jnp.transpose(lax.map(one_frame, frames), (1, 0, 2))
    joined = jnp.concatenate([normed, jnp.broadcast_to(query_features[:, None, :], normed.shape)], axis=-1)
    stream = jnp.dot(joined.reshape(-1, 2 * C), in_weight, preferred_element_type=jnp.float32)
    stream = stream.reshape(QUERIES, FRAMES, D)
    for block_index in range(BLOCKS):
        level = rms_scale(stream, 1e-05).astype(jnp.bfloat16)
        padded = jnp.pad(level, ((0, 0), (1, 1), (0, 0))).astype(jnp.float32)
        taps = conv_weight[block_index]
        mixed_time = taps[0] * padded[:, :-2] + taps[1] * padded[:, 1:-1] + taps[2] * padded[:, 2:]
        stream = stream + mixed_time
        gated = rms_scale(stream, 1e-05).astype(jnp.bfloat16).reshape(-1, D)
        hidden = jax.nn.gelu(jnp.dot(gated, up_weight[block_index], preferred_element_type=jnp.float32)).astype(jnp.bfloat16)
        delta = jnp.dot(hidden, down_weight[block_index], preferred_element_type=jnp.float32)
        stream = stream + delta.reshape(QUERIES, FRAMES, D)
    return stream.astype(jnp.bfloat16)
```

```python
import functools
import math

import jax
import jax.numpy as jnp
from jax import lax
from jax.experimental import pallas as pl
from jax.experimental.pallas import tpu as pltpu
from jax.sharding import PartitionSpec as P

LANES = 128
BF16 = jnp.bfloat16
F32 = jnp.float32
VMEM = pl.BlockSpec(memory_space=pltpu.VMEM)
ANY = pl.BlockSpec(memory_space=pl.ANY)


def dot(a, b):
    return jnp.dot(a, b, preferred_element_type=F32)


def dot_t(a, b):
    return lax.dot_general(a, b, (((1,), (1,)), ((), ())), preferred_element_type=F32)


def my_part(whole, part, parts):
    size = whole.shape[-1] // parts
    mine = whole[:, :size]
    for at in range(1, parts):
        mine = jnp.where(part == at, whole[:, at * size : (at + 1) * size], mine)
    return mine


def inverse_rms(values, epsilon):
    return lax.rsqrt(jnp.mean(values * values, axis=-1, keepdims=True) + epsilon)


def pick_body(parts, frame_ref, pixel_ref, frames_ref, out_ref):
    frame_count, pixel_count, _ = frames_ref.shape
    part = lax.axis_index("split")
    first = lax.axis_index("frame") * frame_count
    side = math.isqrt(pixel_count)
    pixel = pixel_ref[...]
    local = my_part(frame_ref[...], part, parts) - first
    row = my_part(pixel[0:1], part, parts)
    col = my_part(pixel[1:2], part, parts)
    owned = (local >= 0) & (local < frame_count)
    place = jnp.where(owned, local * pixel_count + row * side + col, -1)
    count = place.shape[1]
    place = jnp.transpose(jnp.broadcast_to(place, (8, count)))[:, :1]
    chunk = min(512, pixel_count)
    order = lax.broadcasted_iota(jnp.int32, (count, chunk), 1)
    total = None
    for t in range(frame_count):
        for at in range(0, pixel_count, chunk):
            start = t * pixel_count + at
            hot = jnp.where(order == place - start, 1.0, 0.0).astype(BF16)
            part_sum = dot(hot, frames_ref[t, at : at + chunk, :])
            total = part_sum if total is None else total + part_sum
    out_ref[...] = total.astype(BF16)


def add_body(a_ref, b_ref, out_ref):
    out_ref[...] = a_ref[...] + b_ref[...]


def attend(features, frame_ref, t, scale):
    rows = features.shape[0]
    step = 64
    out = []
    for at in range(0, rows, step):
        scores = dot_t(features[at : at + step], frame_ref[t])
        peak = jnp.max(scores, axis=-1, keepdims=True)
        expd = jnp.exp2((scores - peak) * scale)
        total = jnp.sum(expd, axis=-1, keepdims=True)
        pooled = dot(expd.astype(BF16), frame_ref[t])
        mean = jnp.mean(pooled * pooled, axis=-1, keepdims=True)
        out.append((pooled * lax.rsqrt(mean + 1e-6 * total * total)).astype(BF16))
    return jnp.concatenate(out, axis=0)


def attend_body(scale, a_ref, b_ref, frames_ref, normed_ref, features_ref, near_ref, far_ref):
    frame_count = frames_ref.shape[0]
    features = a_ref[...] + b_ref[...]
    features_ref[...] = features
    for t in range(frame_count):
        normed_ref[t] = attend(features, frames_ref, t, scale)
    even = lax.rem(lax.axis_index("frame"), 2) == 0
    first, last = normed_ref[0], normed_ref[frame_count - 1]
    near_ref[...] = jnp.where(even, last, first)
    far_ref[...] = jnp.where(even, first, last)


def mixer_body(
    devices,
    normed_ref,
    features_ref,
    near_ref,
    far_ref,
    in_ref,
    taps_ref,
    up_a_ref,
    up_b_ref,
    down_a_ref,
    down_b_ref,
    out_ref,
    scratch,
):
    frame_count, rows, channels = normed_ref.shape
    width = in_ref.shape[1]
    place = lax.axis_index("frame")
    even = lax.rem(place, 2) == 0
    near, far = near_ref[...], far_ref[...]
    before = jnp.where(even, far, near)
    after = jnp.where(even, near, far)
    base = dot(features_ref[...], in_ref[channels:, :])

    def stream_of(normed):
        return dot(normed, in_ref[:channels, :]) + base

    def level_of(stream):
        return (stream * inverse_rms(stream, 1e-5)).astype(BF16).astype(F32)

    streams = [stream_of(normed_ref[t]) for t in range(frame_count)]
    levels = [level_of(s) for s in streams]
    left = level_of(stream_of(before)) * (place > 0).astype(F32)
    right = level_of(stream_of(after)) * (place < devices - 1).astype(F32)
    levels = [left] + levels + [right]
    taps = taps_ref[0]
    gated = []
    for t in range(frame_count):
        mixed = (
            taps[0:1] * levels[t] + taps[1:2] * levels[t + 1] + taps[2:3] * levels[t + 2]
        )
        streams[t] = streams[t] + mixed
        gated.append((streams[t] * inverse_rms(streams[t], 1e-5)).astype(BF16))
    gated = jnp.concatenate(gated, axis=0)
    total = jnp.concatenate(streams, axis=0)
    for up_ref, down_ref in ((up_a_ref, down_a_ref), (up_b_ref, down_b_ref)):
        units = up_ref.shape[2]
        step = min(512, units)
        for at in range(0, units, step):
            hidden = jax.nn.gelu(dot(gated, up_ref[0, :, at : at + step])).astype(BF16)
            total = total + dot(hidden, down_ref[0, at : at + step, :])
    blocks = width // LANES
    stride = blocks * frame_count
    for t in range(frame_count):
        for b in range(blocks):
            scratch[pl.ds(b * frame_count + t, rows, stride=stride), :] = total[
                t * rows : (t + 1) * rows, b * LANES : (b + 1) * LANES
            ]
    out_ref[...] = scratch[...].astype(BF16)


def merge_body(own_ref, other_ref, out_ref, sems):
    rows = own_ref.shape[0]
    part = lax.axis_index("split")
    own = pltpu.make_async_copy(own_ref, out_ref.at[pl.ds(part * rows, rows)], sems.at[0])
    other = pltpu.make_async_copy(
        other_ref, out_ref.at[pl.ds((1 - part) * rows, rows)], sems.at[1]
    )
    own.start()
    other.start()
    own.wait()
    other.wait()


def on_device(frames, query_frame, query_pixel, in_weight, conv_weight, up_weight, down_weight):
    frame_count, pixel_count, channels = frames.shape
    query_count = query_frame.shape[0]
    width = in_weight.shape[1]
    parts = lax.axis_size("split")
    devices = lax.axis_size("frame")
    assert parts == 2 and devices & (devices - 1) == 0
    rows = query_count // parts
    swap = [(0, 1), (1, 0)]
    up_other = lax.ppermute(up_weight, "split", swap)
    down_other = lax.ppermute(down_weight, "split", swap)
    shape = jax.ShapeDtypeStruct
    mine = pl.pallas_call(
        functools.partial(pick_body, parts),
        out_shape=shape((rows, channels), BF16),
        in_specs=[VMEM] * 3,
        out_specs=VMEM,
        name="pick",
    )(query_frame.reshape(1, query_count), query_pixel, frames)
    stage = 1
    theirs = None
    while stage < devices:
        if theirs is not None:
            mine = pl.pallas_call(
                add_body,
                out_shape=shape((rows, channels), BF16),
                in_specs=[VMEM] * 2,
                out_specs=VMEM,
                name="join",
            )(mine, theirs)
        flip = 2 * stage - 1
        theirs = lax.ppermute(mine, "frame", [(i, i ^ flip) for i in range(devices)])
        stage *= 2
    scale = math.log2(math.e) / math.sqrt(channels)
    normed, features, near, far = pl.pallas_call(
        functools.partial(attend_body, scale),
        out_shape=(
            shape((frame_count, rows, channels), BF16),
            shape((rows, channels), BF16),
            shape((rows, channels), BF16),
            shape((rows, channels), BF16),
        ),
        in_specs=[VMEM] * 3,
        out_specs=(VMEM,) * 4,
        name="attend",
    )(mine, theirs, frames)
    near = lax.ppermute(near, "frame", [(i, i ^ 1) for i in range(devices)])
    pairs = [(i, i + 1) for i in range(1, devices - 1, 2)]
    far = lax.ppermute(far, "frame", pairs + [(b, a) for a, b in pairs])
    blocks = width // LANES
    lines = rows * blocks * frame_count
    own = pl.pallas_call(
        functools.partial(mixer_body, devices),
        out_shape=shape((lines, LANES), BF16),
        in_specs=[VMEM] * 10,
        out_specs=VMEM,
        scratch_shapes=[pltpu.VMEM((lines, LANES), F32)],
        name="mixer",
    )(
        normed,
        features,
        near,
        far,
        in_weight,
        conv_weight,
        up_weight,
        up_other,
        down_weight,
        down_other,
    )
    other = lax.ppermute(own, "split", swap)
    both = pl.pallas_call(
        merge_body,
        out_shape=shape((parts * lines, LANES), BF16),
        in_specs=[ANY] * 2,
        out_specs=ANY,
        scratch_shapes=[pltpu.SemaphoreType.DMA((2,))],
        name="merge",
    )(own, other)
    both = both.reshape(query_count, blocks, frame_count, LANES)
    return both.transpose(0, 2, 1, 3).reshape(query_count, frame_count, width)


def solution(mesh):
    return jax.shard_map(
        on_device,
        mesh=mesh,
        in_specs=(
            P(("dom", "frame"), None, None),
            P(("dom", "query")),
            P(None, ("dom", "query")),
            P(),
            P(),
            P(None, None, "split"),
            P(None, "split", None),
        ),
        out_specs=P(("dom", "query"), "frame", None),
        check_vma=False,
    )
```

```python
import functools
import math

import jax
import jax.numpy as jnp
from jax import lax
from jax.experimental import pallas as pl
from jax.experimental.pallas import tpu as pltpu
from jax.sharding import PartitionSpec as P

LANES = 128
ROOM = 24 * 1024 * 1024
BF16 = jnp.bfloat16
F32 = jnp.float32
VMEM = pl.BlockSpec(memory_space=pltpu.VMEM)
ANY = pl.BlockSpec(memory_space=pl.ANY)


def held(value):
    return pltpu.with_memory_space_constraint(value, pltpu.VMEM)


def kept(shape, dtype):
    return pltpu.VMEM(shape, dtype)


def dot(a, b):
    return jnp.dot(a, b, preferred_element_type=F32)


def dot_t(a, b):
    return lax.dot_general(a, b, (((1,), (1,)), ((), ())), preferred_element_type=F32)


def my_part(whole, part, parts):
    size = whole.shape[-1] // parts
    mine = whole[:, :size]
    for at in range(1, parts):
        mine = jnp.where(part == at, whole[:, at * size : (at + 1) * size], mine)
    return mine


def inverse_rms(values, epsilon):
    return lax.rsqrt(jnp.mean(values * values, axis=-1, keepdims=True) + epsilon)


def pick_body(parts, frame_ref, pixel_ref, frames_ref, out_ref):
    frame_count, pixel_count, _ = frames_ref.shape
    part = lax.axis_index("split")
    first = lax.axis_index("frame") * frame_count
    side = math.isqrt(pixel_count)
    pixel = pixel_ref[...]
    local = my_part(frame_ref[...], part, parts) - first
    row = my_part(pixel[0:1], part, parts)
    col = my_part(pixel[1:2], part, parts)
    owned = (local >= 0) & (local < frame_count)
    place = jnp.where(owned, local * pixel_count + row * side + col, -1)
    count = place.shape[1]
    place = jnp.transpose(jnp.broadcast_to(place, (8, count)))[:, :1]
    chunk = min(512, pixel_count)
    order = lax.broadcasted_iota(jnp.int32, (count, chunk), 1)
    total = None
    for t in range(frame_count):
        for at in range(0, pixel_count, chunk):
            start = t * pixel_count + at
            hot = jnp.where(order == place - start, 1.0, 0.0).astype(BF16)
            part_sum = dot(hot, frames_ref[t, at : at + chunk, :])
            total = part_sum if total is None else total + part_sum
    out_ref[...] = total.astype(BF16)


def add_body(a_ref, b_ref, out_ref):
    out_ref[...] = a_ref[...] + b_ref[...]


def attend(features, frame_ref, t, scale):
    rows = features.shape[0]
    step = 64
    out = []
    for at in range(0, rows, step):
        scores = dot_t(features[at : at + step], frame_ref[t])
        peak = jnp.max(scores, axis=-1, keepdims=True)
        expd = jnp.exp2((scores - peak) * scale)
        total = jnp.sum(expd, axis=-1, keepdims=True)
        pooled = dot(expd.astype(BF16), frame_ref[t])
        mean = jnp.mean(pooled * pooled, axis=-1, keepdims=True)
        out.append((pooled * lax.rsqrt(mean + 1e-6 * total * total)).astype(BF16))
    return jnp.concatenate(out, axis=0)


def attend_body(scale, a_ref, b_ref, frames_ref, normed_ref, features_ref, near_ref, far_ref):
    frame_count = frames_ref.shape[0]
    features = a_ref[...] + b_ref[...]
    features_ref[...] = features
    for t in range(frame_count):
        normed_ref[t] = attend(features, frames_ref, t, scale)
    even = lax.rem(lax.axis_index("frame"), 2) == 0
    first, last = normed_ref[0], normed_ref[frame_count - 1]
    near_ref[...] = jnp.where(even, last, first)
    far_ref[...] = jnp.where(even, first, last)


def mixer_body(
    devices,
    normed_ref,
    features_ref,
    near_ref,
    far_ref,
    in_ref,
    taps_ref,
    up_a_ref,
    up_b_ref,
    down_a_ref,
    down_b_ref,
    out_ref,
    scratch,
):
    frame_count, rows, channels = normed_ref.shape
    width = in_ref.shape[1]
    place = lax.axis_index("frame")
    even = lax.rem(place, 2) == 0
    near, far = near_ref[...], far_ref[...]
    before = jnp.where(even, far, near)
    after = jnp.where(even, near, far)
    base = dot(features_ref[...], in_ref[channels:, :])

    def stream_of(normed):
        return dot(normed, in_ref[:channels, :]) + base

    def level_of(stream):
        return (stream * inverse_rms(stream, 1e-5)).astype(BF16).astype(F32)

    streams = [stream_of(normed_ref[t]) for t in range(frame_count)]
    levels = [level_of(s) for s in streams]
    left = level_of(stream_of(before)) * (place > 0).astype(F32)
    right = level_of(stream_of(after)) * (place < devices - 1).astype(F32)
    levels = [left] + levels + [right]
    taps = [taps_ref[:, at : at + width] for at in range(0, taps_ref.shape[1], width)]
    gated = []
    for t in range(frame_count):
        mixed = (
            taps[0] * levels[t] + taps[1] * levels[t + 1] + taps[2] * levels[t + 2]
        )
        streams[t] = streams[t] + mixed
        gated.append((streams[t] * inverse_rms(streams[t], 1e-5)).astype(BF16))
    gated = jnp.concatenate(gated, axis=0)
    total = jnp.concatenate(streams, axis=0)
    for up_ref, down_ref in ((up_a_ref, down_a_ref), (up_b_ref, down_b_ref)):
        units = up_ref.shape[2]
        step = min(512, units)
        for at in range(0, units, step):
            hidden = jax.nn.gelu(dot(gated, up_ref[0, :, at : at + step])).astype(BF16)
            total = total + dot(hidden, down_ref[0, at : at + step, :])
    blocks = width // LANES
    stride = blocks * frame_count
    for t in range(frame_count):
        for b in range(blocks):
            scratch[pl.ds(b * frame_count + t, rows, stride=stride), :] = total[
                t * rows : (t + 1) * rows, b * LANES : (b + 1) * LANES
            ]
    out_ref[...] = scratch[...].astype(BF16)


def merge_body(own_ref, other_ref, out_ref, sems):
    rows = own_ref.shape[0]
    part = lax.axis_index("split")
    own = pltpu.make_async_copy(own_ref, out_ref.at[pl.ds(part * rows, rows)], sems.at[0])
    other = pltpu.make_async_copy(
        other_ref, out_ref.at[pl.ds((1 - part) * rows, rows)], sems.at[1]
    )
    own.start()
    other.start()
    own.wait()
    other.wait()


def on_device(frames, query_frame, query_pixel, in_weight, conv_weight, up_weight, down_weight):
    frame_count, pixel_count, channels = frames.shape
    query_count = query_frame.shape[0]
    width = in_weight.shape[1]
    parts = lax.axis_size("split")
    devices = lax.axis_size("frame")
    assert parts == 2 and devices & (devices - 1) == 0
    rows = query_count // parts
    swap = [(0, 1), (1, 0)]
    up_other = held(lax.ppermute(up_weight, "split", swap))
    down_other = held(lax.ppermute(down_weight, "split", swap))
    frames = held(frames)
    mine = pl.pallas_call(
        functools.partial(pick_body, parts),
        out_shape=kept((rows, channels), BF16),
        in_specs=[VMEM] * 3,
        out_specs=VMEM,
        compiler_params=pltpu.CompilerParams(vmem_limit_bytes=ROOM),
        name="pick",
    )(query_frame.reshape(1, query_count), query_pixel, frames)
    stage = 1
    theirs = None
    while stage < devices:
        if theirs is not None:
            mine = pl.pallas_call(
                add_body,
                out_shape=kept((rows, channels), BF16),
                in_specs=[VMEM] * 2,
                out_specs=VMEM,
                compiler_params=pltpu.CompilerParams(vmem_limit_bytes=ROOM),
        name="join",
            )(mine, theirs)
        flip = 2 * stage - 1
        theirs = held(lax.ppermute(mine, "frame", [(i, i ^ flip) for i in range(devices)]))
        stage *= 2
    scale = math.log2(math.e) / math.sqrt(channels)
    normed, features, near, far = pl.pallas_call(
        functools.partial(attend_body, scale),
        out_shape=(
            kept((frame_count, rows, channels), BF16),
            kept((rows, channels), BF16),
            kept((rows, channels), BF16),
            kept((rows, channels), BF16),
        ),
        in_specs=[VMEM] * 3,
        out_specs=(VMEM,) * 4,
        compiler_params=pltpu.CompilerParams(vmem_limit_bytes=ROOM),
        name="attend",
    )(mine, theirs, frames)
    near = held(lax.ppermute(near, "frame", [(i, i ^ 1) for i in range(devices)]))
    pairs = [(i, i + 1) for i in range(1, devices - 1, 2)]
    far = held(lax.ppermute(far, "frame", pairs + [(b, a) for a, b in pairs]))
    blocks = width // LANES
    lines = rows * blocks * frame_count
    own = pl.pallas_call(
        functools.partial(mixer_body, devices),
        out_shape=kept((lines, LANES), BF16),
        in_specs=[VMEM] * 10,
        out_specs=VMEM,
        scratch_shapes=[pltpu.VMEM((lines, LANES), F32)],
        compiler_params=pltpu.CompilerParams(vmem_limit_bytes=ROOM),
        name="mixer",
    )(
        normed,
        features,
        near,
        far,
        held(in_weight),
        held(conv_weight.reshape(1, conv_weight.shape[1] * width)),
        held(up_weight),
        up_other,
        held(down_weight),
        down_other,
    )
    other = held(lax.ppermute(own, "split", swap))
    both = pl.pallas_call(
        merge_body,
        out_shape=jax.ShapeDtypeStruct((parts * lines, LANES), BF16),
        in_specs=[VMEM] * 2,
        out_specs=ANY,
        scratch_shapes=[pltpu.SemaphoreType.DMA((2,))],
        compiler_params=pltpu.CompilerParams(vmem_limit_bytes=ROOM),
        name="merge",
    )(own, other)
    both = both.reshape(query_count, blocks, frame_count, LANES)
    return both.transpose(0, 2, 1, 3).reshape(query_count, frame_count, width)


def solution(mesh):
    return jax.shard_map(
        on_device,
        mesh=mesh,
        in_specs=(
            P(("dom", "frame"), None, None),
            P(("dom", "query")),
            P(None, ("dom", "query")),
            P(),
            P(),
            P(None, None, "split"),
            P(None, "split", None),
        ),
        out_specs=P(("dom", "query"), "frame", None),
        check_vma=False,
    )
```

```python
import functools
import math

import jax
import jax.numpy as jnp
from jax import lax
from jax.experimental import pallas as pl
from jax.experimental.pallas import tpu as pltpu
from jax.sharding import PartitionSpec as P

LANES = 128
ROOM = 20 * 1024 * 1024
BF16 = jnp.bfloat16
F32 = jnp.float32
VMEM = pl.BlockSpec(memory_space=pltpu.VMEM)
HBM = pl.BlockSpec(memory_space=pltpu.HBM)


def held(value):
    return pltpu.with_memory_space_constraint(value, pltpu.VMEM)


def fixed(value):
    return pltpu.with_memory_space_constraint(value, pltpu.HBM)


def kept(shape, dtype):
    return pltpu.VMEM(shape, dtype)


def call(body, name, out, count, scratch=(), in_specs=None, out_specs=None):
    many = isinstance(out, tuple)
    if out_specs is None:
        out_specs = (VMEM,) * len(out) if many else VMEM
    return pl.pallas_call(
        body,
        out_shape=out,
        in_specs=[VMEM] * count if in_specs is None else in_specs,
        out_specs=out_specs,
        scratch_shapes=list(scratch),
        compiler_params=pltpu.CompilerParams(vmem_limit_bytes=ROOM),
        name=name,
    )


def dot(a, b):
    return jnp.dot(a, b, preferred_element_type=F32)


def dot_t(a, b):
    return lax.dot_general(a, b, (((1,), (1,)), ((), ())), preferred_element_type=F32)


def my_part(whole, part, parts):
    size = whole.shape[-1] // parts
    mine = whole[:, :size]
    for at in range(1, parts):
        mine = jnp.where(part == at, whole[:, at * size : (at + 1) * size], mine)
    return mine


def is_even():
    return lax.rem(lax.axis_index("frame"), 2) == 0


def near_frame():
    return 1 - lax.rem(lax.axis_index("frame"), 2)


def inverse_rms(values, epsilon):
    return lax.rsqrt(jnp.mean(values * values, axis=-1, keepdims=True) + epsilon)


def level_of(stream):
    return (stream * inverse_rms(stream, 1e-5)).astype(BF16).astype(F32)


def pick_body(parts, frame_hbm, pixel_hbm, frames_hbm, out_ref, frame_ref, pixel_ref, frames_ref, sems):
    frame_count, pixel_count, _ = frames_ref.shape
    loads = [
        pltpu.make_async_copy(frame_hbm, frame_ref, sems.at[0]),
        pltpu.make_async_copy(pixel_hbm, pixel_ref, sems.at[1]),
    ]
    maps = [
        pltpu.make_async_copy(frames_hbm.at[t], frames_ref.at[t], sems.at[2 + t])
        for t in range(frame_count)
    ]
    for copy in loads + maps:
        copy.start()
    for copy in loads:
        copy.wait()
    part = lax.axis_index("split")
    first = lax.axis_index("frame") * frame_count
    side = math.isqrt(pixel_count)
    pixel = pixel_ref[...]
    local = my_part(frame_ref[...], part, parts) - first
    row = my_part(pixel[0:1], part, parts)
    col = my_part(pixel[1:2], part, parts)
    owned = (local >= 0) & (local < frame_count)
    place = jnp.where(owned, local * pixel_count + row * side + col, -1)
    count = place.shape[1]
    place = jnp.transpose(jnp.broadcast_to(place, (8, count)))[:, :1]
    chunk = min(512, pixel_count)
    order = lax.broadcasted_iota(jnp.int32, (count, chunk), 1)
    total = None
    for t in range(frame_count):
        maps[t].wait()
        for at in range(0, pixel_count, chunk):
            start = t * pixel_count + at
            hot = jnp.where(order == place - start, 1.0, 0.0).astype(BF16)
            part_sum = dot(hot, frames_ref[t, at : at + chunk, :])
            total = part_sum if total is None else total + part_sum
    out_ref[...] = total.astype(BF16)


def join_body(a_ref, b_ref, out_ref):
    out_ref[...] = a_ref[...] + b_ref[...]


def attend(features, frames_ref, t, scale, score_ref, weight_ref, sum_ref):
    rows = features.shape[0]
    pixel_count = frames_ref.shape[1]
    chunk = min(256, pixel_count)
    step = 32
    for at in range(0, pixel_count, chunk):
        score_ref[:, at : at + chunk] = dot_t(features, frames_ref[t, at : at + chunk, :])
    for at in range(0, rows, step):
        scores = score_ref[at : at + step, :]
        peak = jnp.max(scores, axis=-1, keepdims=True)
        expd = jnp.exp2((scores - peak) * scale)
        total = jnp.sum(expd, axis=-1, keepdims=True)
        sum_ref[at : at + step, :] = jnp.broadcast_to(total, (step, LANES))
        weight_ref[at : at + step, :] = expd.astype(BF16)
    pooled = dot(weight_ref[...], frames_ref[t])
    total = sum_ref[:, :1]
    mean = jnp.mean(pooled * pooled, axis=-1, keepdims=True)
    return (pooled * lax.rsqrt(mean + 1e-6 * total * total)).astype(BF16)


def near_body(scale, a_ref, b_ref, frames_ref, features_ref, normed_ref, *scratch):
    features = a_ref[...] + b_ref[...]
    features_ref[...] = features
    normed_ref[...] = attend(features, frames_ref, near_frame(), scale, *scratch)


def far_body(scale, features_ref, frames_ref, normed_ref, *scratch):
    normed_ref[...] = attend(features_ref[...], frames_ref, 1 - near_frame(), scale, *scratch)


def taps_of(taps_ref):
    width = taps_ref.shape[1] // 3
    first, middle, last = (taps_ref[:, k * width : (k + 1) * width] for k in range(3))
    even = is_even()
    return jnp.where(even, last, first), middle, jnp.where(even, first, last)


def own_body(features_ref, near_ref, far_ref, in_ref, taps_ref, base_ref, near_out, far_out):
    channels = features_ref.shape[1]
    near_tap, middle, far_tap = taps_of(taps_ref)
    base = dot(features_ref[...], in_ref[channels:, :])
    base_ref[...] = base
    near = dot(near_ref[...], in_ref[:channels, :]) + base
    far = dot(far_ref[...], in_ref[:channels, :]) + base
    near_level, far_level = level_of(near), level_of(far)
    near_out[...] = near + middle * near_level + far_tap * far_level
    far_out[...] = far + middle * far_level + near_tap * near_level


def mix(stream, ups, downs, hidden_ref):
    gated = (stream * inverse_rms(stream, 1e-5)).astype(BF16)
    base = 0
    total = None
    for up_ref, down_ref in zip(ups, downs):
        units = up_ref.shape[2]
        step = min(256, units)
        for at in range(0, units, step):
            x = dot(gated, up_ref[0, :, at : at + step])
            inner = x * (x * x * (0.044715 * math.sqrt(2 / math.pi)) + math.sqrt(2 / math.pi))
            hidden_ref[:, base + at : base + at + step] = (x + x * jnp.tanh(inner)).astype(BF16)
        base += units
    base = 0
    for up_ref, down_ref in zip(ups, downs):
        units = up_ref.shape[2]
        part = dot(hidden_ref[:, base : base + units], down_ref[0])
        total = part if total is None else total + part
        base += units
    return stream + 0.5 * total


def mixed_stream(halo_ref, own_ref, base_ref, in_ref, tap, inside):
    channels = halo_ref.shape[1]
    halo = level_of(dot(halo_ref[...], in_ref[:channels, :]) + base_ref[...])
    return own_ref[...] + jnp.where(inside, tap, 0.0) * halo


def mix_near_body(
    devices, halo_ref, own_ref, base_ref, in_ref, taps_ref, up_a, up_b, down_a, down_b, out_ref, hidden_ref
):
    place = lax.axis_index("frame")
    inside = jnp.logical_not(is_even()) | (place < devices - 1)
    tap, _, _ = taps_of(taps_ref)
    stream = mixed_stream(halo_ref, own_ref, base_ref, in_ref, tap, inside)
    out_ref[...] = mix(stream, (up_a, up_b), (down_a, down_b), hidden_ref)


def mix_far_body(
    devices,
    halo_ref,
    own_ref,
    base_ref,
    in_ref,
    taps_ref,
    up_a,
    up_b,
    down_a,
    down_b,
    near_ref,
    out_ref,
    hidden_ref,
    line_ref,
):
    place = lax.axis_index("frame")
    even = is_even()
    inside = jnp.where(even, place > 0, place < devices - 1)
    _, _, tap = taps_of(taps_ref)
    stream = mixed_stream(halo_ref, own_ref, base_ref, in_ref, tap, inside)
    far = mix(stream, (up_a, up_b), (down_a, down_b), hidden_ref)
    near = near_ref[...]
    rows, width = far.shape
    blocks = width // LANES
    for t, value in ((0, jnp.where(even, far, near)), (1, jnp.where(even, near, far))):
        for b in range(blocks):
            line_ref[pl.ds(b * 2 + t, rows, stride=blocks * 2), :] = value[
                :, b * LANES : (b + 1) * LANES
            ]
    out_ref[...] = line_ref[...].astype(BF16)


def merge_body(own_ref, other_ref, out_ref, sems):
    rows = own_ref.shape[0]
    part = lax.axis_index("split")
    own = pltpu.make_async_copy(own_ref, out_ref.at[pl.ds(part * rows, rows)], sems.at[0])
    other = pltpu.make_async_copy(
        other_ref, out_ref.at[pl.ds((1 - part) * rows, rows)], sems.at[1]
    )
    own.start()
    other.start()
    own.wait()
    other.wait()


def on_device(frames, query_frame, query_pixel, in_weight, conv_weight, up_weight, down_weight):
    frame_count, pixel_count, channels = frames.shape
    query_count = query_frame.shape[0]
    width = in_weight.shape[1]
    units = up_weight.shape[2]
    parts = lax.axis_size("split")
    devices = lax.axis_size("frame")
    assert parts == 2 and frame_count == 2 and devices > 1 and devices & (devices - 1) == 0
    rows = query_count // parts
    swap = [(0, 1), (1, 0)]
    flips = lambda mask: [(i, i ^ mask) for i in range(devices)]
    up_other = held(lax.ppermute(up_weight, "split", swap))
    down_other = held(lax.ppermute(down_weight, "split", swap))
    mine = call(
        functools.partial(pick_body, parts),
        "pick",
        kept((rows, channels), BF16),
        3,
        scratch=(
            pltpu.VMEM((1, query_count), jnp.int32),
            pltpu.VMEM(query_pixel.shape, jnp.int32),
            pltpu.VMEM(frames.shape, BF16),
            pltpu.SemaphoreType.DMA((2 + frame_count,)),
        ),
        in_specs=[HBM] * 3,
    )(*(fixed(x) for x in (query_frame.reshape(1, query_count), query_pixel, frames)))
    theirs = held(lax.ppermute(mine, "frame", flips(1)))
    stage = 2
    while stage < devices:
        mine = call(join_body, "join", kept((rows, channels), BF16), 2)(mine, theirs)
        theirs = held(lax.ppermute(mine, "frame", flips(2 * stage - 1)))
        stage *= 2
    frames = held(frames)
    in_weight = held(in_weight)
    taps = held(conv_weight.reshape(1, conv_weight.shape[1] * width))
    weights = (held(up_weight), up_other, held(down_weight), down_other)
    scale = math.log2(math.e) / math.sqrt(channels)
    attention_scratch = (
        pltpu.VMEM((rows, pixel_count), F32),
        pltpu.VMEM((rows, pixel_count), BF16),
        pltpu.VMEM((rows, LANES), F32),
    )
    small = kept((rows, channels), BF16)
    wide = kept((rows, width), F32)
    features, near = call(
        functools.partial(near_body, scale), "near", (small, small), 3, attention_scratch
    )(mine, theirs, frames)
    near_halo = held(lax.ppermute(near, "frame", flips(1)))
    far = call(functools.partial(far_body, scale), "far", small, 2, attention_scratch)(
        features, frames
    )
    pairs = [(i, i + 1) for i in range(1, devices - 1, 2)]
    far_halo = held(lax.ppermute(far, "frame", pairs + [(b, a) for a, b in pairs]))
    base, own_near, own_far = call(own_body, "own", (wide,) * 3, 5)(
        features, near, far, in_weight, taps
    )
    hidden = pltpu.VMEM((rows, parts * units), BF16)
    near = call(functools.partial(mix_near_body, devices), "mix_near", wide, 9, (hidden,))(
        near_halo, own_near, base, in_weight, taps, *weights
    )
    blocks = width // LANES
    lines = rows * blocks * frame_count
    own = call(
        functools.partial(mix_far_body, devices),
        "mix_far",
        kept((lines, LANES), BF16),
        10,
        (hidden, pltpu.VMEM((lines, LANES), F32)),
    )(far_halo, own_far, base, in_weight, taps, *weights, near)
    other = held(lax.ppermute(own, "split", swap))
    both = call(
        merge_body,
        "merge",
        jax.ShapeDtypeStruct((parts * lines, LANES), BF16),
        2,
        (pltpu.SemaphoreType.DMA((2,)),),
        out_specs=HBM,
    )(own, other)
    both = both.reshape(query_count, blocks, frame_count, LANES)
    return both.transpose(0, 2, 1, 3).reshape(query_count, frame_count, width)


def solution(mesh):
    return jax.shard_map(
        on_device,
        mesh=mesh,
        in_specs=(
            P(("dom", "frame"), None, None),
            P(("dom", "query")),
            P(None, ("dom", "query")),
            P(),
            P(),
            P(None, None, "split"),
            P(None, "split", None),
        ),
        out_specs=P(("dom", "query"), "frame", None),
        check_vma=False,
    )
```

```python
import functools
import math

import jax
import jax.numpy as jnp
from jax import lax
from jax.experimental import pallas as pl
from jax.experimental.pallas import tpu as pltpu
from jax.sharding import PartitionSpec as P


LANES = 128
ROOM = 20 * 1024 * 1024
BF16 = jnp.bfloat16
F32 = jnp.float32
VMEM = pl.BlockSpec(memory_space=pltpu.VMEM)
HBM = pl.BlockSpec(memory_space=pltpu.HBM)


def held(value):
    return pltpu.with_memory_space_constraint(value, pltpu.VMEM)


def fixed(value):
    return pltpu.with_memory_space_constraint(value, pltpu.HBM)


def kept(shape, dtype):
    return pltpu.VMEM(shape, dtype)


def call(body, out, count, scratch=(), in_specs=None, out_specs=None, aliases=None):
    many = isinstance(out, tuple)
    if out_specs is None:
        out_specs = (VMEM,) * len(out) if many else VMEM
    return pl.pallas_call(
        body,
        out_shape=out,
        in_specs=[VMEM] * count if in_specs is None else in_specs,
        out_specs=out_specs,
        scratch_shapes=list(scratch),
        input_output_aliases=aliases or {},
        compiler_params=pltpu.CompilerParams(vmem_limit_bytes=ROOM),
    )


def dot(a, b):
    return jnp.dot(a, b, preferred_element_type=F32)


def dot_t(a, b):
    return lax.dot_general(a, b, (((1,), (1,)), ((), ())), preferred_element_type=F32)


def my_part(whole, part, parts):
    size = whole.shape[-1] // parts
    mine = whole[:, :size]
    for at in range(1, parts):
        mine = jnp.where(part == at, whole[:, at * size : (at + 1) * size], mine)
    return mine


def is_even():
    return lax.rem(lax.axis_index("frame"), 2) == 0


def near_frame():
    return 1 - lax.rem(lax.axis_index("frame"), 2)


def inverse_rms(values, epsilon):
    return lax.rsqrt(jnp.mean(values * values, axis=-1, keepdims=True) + epsilon)


def level_of(stream):
    return (stream * inverse_rms(stream, 1e-5)).astype(BF16).astype(F32)


def pick_body(
    parts, frame_hbm, pixel_hbm, frames_hbm, out_ref, frames_ref, frame_ref, pixel_ref, sems
):
    frame_count, pixel_count, _ = frames_ref.shape
    loads = [
        pltpu.make_async_copy(frame_hbm, frame_ref, sems.at[0]),
        pltpu.make_async_copy(pixel_hbm, pixel_ref, sems.at[1]),
    ]
    chunk = min(512, pixel_count)
    spots = [(t, at) for t in range(frame_count) for at in range(0, pixel_count, chunk)]
    maps = [
        pltpu.make_async_copy(
            frames_hbm.at[t, pl.ds(at, chunk)], frames_ref.at[t, pl.ds(at, chunk)], sems.at[2 + k]
        )
        for k, (t, at) in enumerate(spots)
    ]
    for copy in loads + maps:
        copy.start()
    for copy in loads:
        copy.wait()
    part = lax.axis_index("split")
    first = lax.axis_index("frame") * frame_count
    side = math.isqrt(pixel_count)
    pixel = pixel_ref[...]
    local = my_part(frame_ref[...], part, parts) - first
    row = my_part(pixel[0:1], part, parts)
    col = my_part(pixel[1:2], part, parts)
    owned = (local >= 0) & (local < frame_count)
    place = jnp.where(owned, local * pixel_count + row * side + col, -1)
    count = place.shape[1]
    place = jnp.transpose(jnp.broadcast_to(place, (8, count)))[:, :1]
    order = lax.broadcasted_iota(jnp.int32, (count, chunk), 1)
    total = None
    for copy, (t, at) in zip(maps, spots):
        hot = jnp.where(order == place - (t * pixel_count + at), 1.0, 0.0).astype(BF16)
        copy.wait()
        part_sum = dot(hot, frames_ref[t, at : at + chunk, :])
        total = part_sum if total is None else total + part_sum
    out_ref[...] = total.astype(BF16)


def join_body(a_ref, b_ref, out_ref):
    out_ref[...] = a_ref[...] + b_ref[...]


def attend(features, frames_ref, t, scale, score_ref, weight_ref, sum_ref):
    rows = features.shape[0]
    pixel_count = frames_ref.shape[1]
    chunk = min(256, pixel_count)
    step = 32
    for at in range(0, pixel_count, chunk):
        score_ref[:, at : at + chunk] = dot_t(features, frames_ref[t, at : at + chunk, :])
    for at in range(0, rows, step):
        scores = score_ref[at : at + step, :]
        peak = jnp.max(scores, axis=-1, keepdims=True)
        expd = jnp.exp2((scores - peak) * scale)
        total = jnp.sum(expd, axis=-1, keepdims=True)
        sum_ref[at : at + step, :] = jnp.broadcast_to(total, (step, LANES))
        weight_ref[at : at + step, :] = expd.astype(BF16)
    pooled = dot(weight_ref[...], frames_ref[t])
    total = sum_ref[:, :1]
    mean = jnp.mean(pooled * pooled, axis=-1, keepdims=True)
    return (pooled * lax.rsqrt(mean + 1e-6 * total * total)).astype(BF16)


def near_body(scale, a_ref, b_ref, frames_ref, features_ref, normed_ref, *scratch):
    features = a_ref[...] + b_ref[...]
    features_ref[...] = features
    normed_ref[...] = attend(features, frames_ref, near_frame(), scale, *scratch)


def far_body(scale, features_ref, frames_ref, normed_ref, *scratch):
    normed_ref[...] = attend(features_ref[...], frames_ref, 1 - near_frame(), scale, *scratch)


def taps_of(taps_ref):
    width = taps_ref.shape[1] // 3
    first, middle, last = (taps_ref[:, k * width : (k + 1) * width] for k in range(3))
    even = is_even()
    return jnp.where(even, last, first), middle, jnp.where(even, first, last)


def own_body(features_ref, near_ref, far_ref, in_ref, taps_ref, base_ref, near_out, far_out):
    channels = features_ref.shape[1]
    near_tap, middle, far_tap = taps_of(taps_ref)
    base = dot(features_ref[...], in_ref[channels:, :])
    base_ref[...] = base
    near = dot(near_ref[...], in_ref[:channels, :]) + base
    far = dot(far_ref[...], in_ref[:channels, :]) + base
    near_level, far_level = level_of(near), level_of(far)
    near_out[...] = near + middle * near_level + far_tap * far_level
    far_out[...] = far + middle * far_level + near_tap * near_level


def mix(stream, ups, downs, hidden_ref):
    gated = (stream * inverse_rms(stream, 1e-5)).astype(BF16)
    base = 0
    total = None
    for up_ref, down_ref in zip(ups, downs):
        units = up_ref.shape[2]
        step = min(256, units)
        for at in range(0, units, step):
            x = dot(gated, up_ref[0, :, at : at + step])
            inner = x * (x * x * (0.044715 * math.sqrt(2 / math.pi)) + math.sqrt(2 / math.pi))
            hidden_ref[:, base + at : base + at + step] = (x + x * jnp.tanh(inner)).astype(BF16)
        base += units
    base = 0
    for up_ref, down_ref in zip(ups, downs):
        units = up_ref.shape[2]
        part = dot(hidden_ref[:, base : base + units], down_ref[0])
        total = part if total is None else total + part
        base += units
    return stream + 0.5 * total


def mixed_stream(halo_ref, own_ref, base_ref, in_ref, tap, inside):
    channels = halo_ref.shape[1]
    halo = level_of(dot(halo_ref[...], in_ref[:channels, :]) + base_ref[...])
    return own_ref[...] + jnp.where(inside, tap, 0.0) * halo


def mix_near_body(
    devices, halo_ref, own_ref, base_ref, in_ref, taps_ref, up_a, up_b, down_a, down_b, out_ref, hidden_ref
):
    place = lax.axis_index("frame")
    inside = jnp.logical_not(is_even()) | (place < devices - 1)
    tap, _, _ = taps_of(taps_ref)
    stream = mixed_stream(halo_ref, own_ref, base_ref, in_ref, tap, inside)
    out_ref[...] = mix(stream, (up_a, up_b), (down_a, down_b), hidden_ref)


def mix_far_body(
    devices,
    halo_ref,
    own_ref,
    base_ref,
    in_ref,
    taps_ref,
    up_a,
    up_b,
    down_a,
    down_b,
    near_ref,
    out_ref,
    hidden_ref,
    line_ref,
):
    place = lax.axis_index("frame")
    even = is_even()
    inside = jnp.where(even, place > 0, place < devices - 1)
    _, _, tap = taps_of(taps_ref)
    stream = mixed_stream(halo_ref, own_ref, base_ref, in_ref, tap, inside)
    far = mix(stream, (up_a, up_b), (down_a, down_b), hidden_ref)
    near = near_ref[...]
    rows, width = far.shape
    blocks = width // LANES
    for t, value in ((0, jnp.where(even, far, near)), (1, jnp.where(even, near, far))):
        for b in range(blocks):
            line_ref[pl.ds(b * 2 + t, rows, stride=blocks * 2), :] = value[
                :, b * LANES : (b + 1) * LANES
            ]
    out_ref[...] = line_ref[...].astype(BF16)


def copy_lines(source_ref, target_ref, first, sems):
    rows = source_ref.shape[0]
    count = sems.shape[0]
    size = rows // count
    copies = [
        pltpu.make_async_copy(
            source_ref.at[pl.ds(k * size, size)],
            target_ref.at[pl.ds(first + k * size, size)],
            sems.at[k],
        )
        for k in range(count)
    ]
    for copy in copies:
        copy.start()
    for copy in copies:
        copy.wait()


def place_body(own_ref, out_ref, sems):
    copy_lines(own_ref, out_ref, lax.axis_index("split") * own_ref.shape[0], sems)


def merge_body(other_ref, _, out_ref, sems):
    copy_lines(other_ref, out_ref, (1 - lax.axis_index("split")) * other_ref.shape[0], sems)


def on_device(frames, query_frame, query_pixel, in_weight, conv_weight, up_weight, down_weight):
    frame_count, pixel_count, channels = frames.shape
    query_count = query_frame.shape[0]
    width = in_weight.shape[1]
    units = up_weight.shape[2]
    parts = lax.axis_size("split")
    devices = lax.axis_size("frame")
    assert parts == 2 and frame_count == 2 and devices > 1 and devices & (devices - 1) == 0
    rows = query_count // parts
    swap = [(0, 1), (1, 0)]
    flips = lambda mask: [(i, i ^ mask) for i in range(devices)]
    mine, frames = call(
        functools.partial(pick_body, parts),
        (kept((rows, channels), BF16), kept(frames.shape, BF16)),
        3,
        scratch=(
            pltpu.VMEM((1, query_count), jnp.int32),
            pltpu.VMEM(query_pixel.shape, jnp.int32),
            pltpu.SemaphoreType.DMA((2 + frame_count * pixel_count // min(512, pixel_count),)),
        ),
        in_specs=[HBM] * 3,
    )(*(fixed(x) for x in (query_frame.reshape(1, query_count), query_pixel, frames)))
    theirs = lax.ppermute(mine, "frame", flips(1))
    up_other = lax.ppermute(up_weight, "split", swap)
    down_other = lax.ppermute(down_weight, "split", swap)
    theirs, up_other, down_other = held(theirs), held(up_other), held(down_other)
    stage = 2
    while stage < devices:
        mine = call(join_body, kept((rows, channels), BF16), 2)(mine, theirs)
        theirs = held(lax.ppermute(mine, "frame", flips(2 * stage - 1)))
        stage *= 2
    in_weight = held(in_weight)
    taps = held(conv_weight.reshape(1, conv_weight.shape[1] * width))
    weights = (held(up_weight), up_other, held(down_weight), down_other)
    scale = math.log2(math.e) / math.sqrt(channels)
    attention_scratch = (
        pltpu.VMEM((rows, pixel_count), F32),
        pltpu.VMEM((rows, pixel_count), BF16),
        pltpu.VMEM((rows, LANES), F32),
    )
    small = kept((rows, channels), BF16)
    wide = kept((rows, width), F32)
    features, near = call(
        functools.partial(near_body, scale), (small, small), 3, attention_scratch
    )(mine, theirs, frames)
    near_halo = held(lax.ppermute(near, "frame", flips(1)))
    far = call(functools.partial(far_body, scale), small, 2, attention_scratch)(features, frames)
    pairs = [
        (parts * i + c, parts * (i + 1) + c) for i in range(1, devices - 1, 2) for c in range(parts)
    ] + [(parts * i, parts * i + 1) for i in (0, devices - 1)]
    far_halo = held(
        lax.ppermute(far, ("frame", "split"), pairs + [(b, a) for a, b in pairs])
    )
    base, own_near, own_far = call(own_body, (wide,) * 3, 5)(features, near, far, in_weight, taps)
    hidden = pltpu.VMEM((rows, parts * units), BF16)
    near = call(functools.partial(mix_near_body, devices), wide, 9, (hidden,))(
        near_halo, own_near, base, in_weight, taps, *weights
    )
    blocks = width // LANES
    lines = rows * blocks * frame_count
    own = call(
        functools.partial(mix_far_body, devices),
        kept((lines, LANES), BF16),
        10,
        (hidden, pltpu.VMEM((lines, LANES), F32)),
    )(far_halo, own_far, base, in_weight, taps, *weights, near)
    other = held(lax.ppermute(own, "split", swap))
    whole = jax.ShapeDtypeStruct((parts * lines, LANES), BF16)
    moves = (pltpu.SemaphoreType.DMA((4,)),)
    both = call(place_body, whole, 1, moves, out_specs=HBM)(own)
    both = call(
        merge_body, whole, 2, moves, in_specs=[VMEM, HBM], out_specs=HBM, aliases={1: 0}
    )(other, both)
    both = both.reshape(query_count, blocks, frame_count, LANES)
    return both.transpose(0, 2, 1, 3).reshape(query_count, frame_count, width)


def solution(mesh):
    return jax.shard_map(
        on_device,
        mesh=mesh,
        in_specs=(
            P(("dom", "frame"), None, None),
            P(("dom", "query")),
            P(None, ("dom", "query")),
            P(),
            P(),
            P(None, None, "split"),
            P(None, "split", None),
        ),
        out_specs=P(("dom", "query"), "frame", None),
        check_vma=False,
    )
```

```python
import functools
import math

import jax
import jax.numpy as jnp
from jax import lax
from jax.experimental import pallas as pl
from jax.experimental.pallas import tpu as pltpu
from jax.sharding import PartitionSpec as P


LANES = 128
ROOM = 20 * 1024 * 1024
BF16 = jnp.bfloat16
F32 = jnp.float32
VMEM = pl.BlockSpec(memory_space=pltpu.VMEM)
HBM = pl.BlockSpec(memory_space=pltpu.HBM)


def held(value):
    return pltpu.with_memory_space_constraint(value, pltpu.VMEM)


def fixed(value):
    return pltpu.with_memory_space_constraint(value, pltpu.HBM)


def kept(shape, dtype):
    return pltpu.VMEM(shape, dtype)


def call(body, out, count, scratch=(), in_specs=None, out_specs=None, aliases=None):
    many = isinstance(out, tuple)
    if out_specs is None:
        out_specs = (VMEM,) * len(out) if many else VMEM
    return pl.pallas_call(
        body,
        out_shape=out,
        in_specs=[VMEM] * count if in_specs is None else in_specs,
        out_specs=out_specs,
        scratch_shapes=list(scratch),
        input_output_aliases=aliases or {},
        compiler_params=pltpu.CompilerParams(vmem_limit_bytes=ROOM),
    )


def dot(a, b):
    return jnp.dot(a, b, preferred_element_type=F32)


def dot_t(a, b):
    return lax.dot_general(a, b, (((1,), (1,)), ((), ())), preferred_element_type=F32)


def my_part(whole, part, parts):
    size = whole.shape[-1] // parts
    mine = whole[:, :size]
    for at in range(1, parts):
        mine = jnp.where(part == at, whole[:, at * size : (at + 1) * size], mine)
    return mine


def is_even():
    return lax.rem(lax.axis_index("frame"), 2) == 0


def near_frame():
    return 1 - lax.rem(lax.axis_index("frame"), 2)


def inverse_rms(values, epsilon):
    return lax.rsqrt(jnp.mean(values * values, axis=-1, keepdims=True) + epsilon)


def level_of(stream):
    return (stream * inverse_rms(stream, 1e-5)).astype(BF16).astype(F32)


def pick_body(
    parts,
    frame_hbm,
    pixel_hbm,
    frames_hbm,
    out_ref,
    frames_ref,
    outer_ref,
    frame_ref,
    pixel_ref,
    sems,
):
    frame_count, pixel_count, _ = frames_ref.shape
    loads = [
        pltpu.make_async_copy(frame_hbm, frame_ref, sems.at[0]),
        pltpu.make_async_copy(pixel_hbm, pixel_ref, sems.at[1]),
    ]
    chunk = min(512, pixel_count)
    spots = [(t, at) for t in range(frame_count) for at in range(0, pixel_count, chunk)]
    maps = [
        pltpu.make_async_copy(
            frames_hbm.at[t, pl.ds(at, chunk)], frames_ref.at[t, pl.ds(at, chunk)], sems.at[2 + k]
        )
        for k, (t, at) in enumerate(spots)
    ]
    part = lax.axis_index("split")
    share = outer_ref.shape[0]
    side_of_pair = lax.rem(lax.axis_index("query"), 2)
    outer = pltpu.make_async_copy(
        frames_hbm.at[1 - near_frame(), pl.ds((2 * part + side_of_pair) * share, share)], outer_ref, sems.at[2 + len(maps)]
    )
    for copy in loads + maps + [outer]:
        copy.start()
    for copy in loads:
        copy.wait()
    first = lax.axis_index("frame") * frame_count
    side = math.isqrt(pixel_count)
    pixel = pixel_ref[...]
    local = my_part(frame_ref[...], part, parts) - first
    row = my_part(pixel[0:1], part, parts)
    col = my_part(pixel[1:2], part, parts)
    owned = (local >= 0) & (local < frame_count)
    place = jnp.where(owned, local * pixel_count + row * side + col, -1)
    count = place.shape[1]
    place = jnp.transpose(jnp.broadcast_to(place, (8, count)))[:, :1]
    order = lax.broadcasted_iota(jnp.int32, (count, chunk), 1)
    total = None
    for copy, (t, at) in zip(maps, spots):
        hot = jnp.where(order == place - (t * pixel_count + at), 1.0, 0.0).astype(BF16)
        copy.wait()
        part_sum = dot(hot, frames_ref[t, at : at + chunk, :])
        total = part_sum if total is None else total + part_sum
    out_ref[...] = total.astype(BF16)
    outer.wait()


def join_body(a_ref, b_ref, out_ref):
    out_ref[...] = a_ref[...] + b_ref[...]


def attend(features, maps, scale, scratch):
    score_ref, weight_ref, sum_ref = scratch
    rows = features.shape[0]
    step = 32
    for k, blocks in enumerate(maps):
        at = 0
        for block in blocks:
            score_ref[k, :, at : at + block.shape[0]] = dot_t(features, block[...])
            at += block.shape[0]
    for k in range(len(maps)):
        for at in range(0, rows, step):
            scores = score_ref[k, at : at + step, :]
            peak = jnp.max(scores, axis=-1, keepdims=True)
            expd = jnp.exp2((scores - peak) * scale)
            total = jnp.sum(expd, axis=-1, keepdims=True)
            sum_ref[k, at : at + step, :] = jnp.broadcast_to(total, (step, LANES))
            weight_ref[k, at : at + step, :] = expd.astype(BF16)
    out = []
    for k, blocks in enumerate(maps):
        at = 0
        pooled = None
        for block in blocks:
            part = dot(weight_ref[k, :, at : at + block.shape[0]], block[...])
            pooled = part if pooled is None else pooled + part
            at += block.shape[0]
        total = sum_ref[k, :, :1]
        mean = jnp.mean(pooled * pooled, axis=-1, keepdims=True)
        out.append((pooled * lax.rsqrt(mean + 1e-6 * total * total)).astype(BF16))
    return out


def near_body(scale, a_ref, b_ref, frames_ref, features_ref, normed_ref, *scratch):
    features = a_ref[...] + b_ref[...]
    features_ref[...] = features
    (normed_ref[...],) = attend(features, [[frames_ref.at[near_frame()]]], scale, scratch)


def far_body(scale, features_ref, frames_ref, normed_ref, *scratch):
    maps = [[frames_ref.at[1 - near_frame()]]]
    (normed_ref[...],) = attend(features_ref[...], maps, scale, scratch)


def taps_of(taps_ref):
    width = taps_ref.shape[1] // 3
    first, middle, last = (taps_ref[:, k * width : (k + 1) * width] for k in range(3))
    even = is_even()
    return jnp.where(even, last, first), middle, jnp.where(even, first, last)


def own_body(
    devices,
    scale,
    features_ref,
    near_ref,
    far_ref,
    a_ref,
    b_ref,
    c_ref,
    d_ref,
    in_ref,
    taps_ref,
    base_ref,
    near_out,
    far_out,
    *scratch,
):
    features = features_ref[...]
    channels = features.shape[1]
    near_tap, middle, far_tap = taps_of(taps_ref)
    place = lax.axis_index("frame")
    inside = jnp.where(is_even(), place > 0, place < devices - 1)
    base = dot(features, in_ref[channels:, :])
    base_ref[...] = base
    near = dot(near_ref[...], in_ref[:channels, :]) + base
    far = dot(far_ref[...], in_ref[:channels, :]) + base
    near_level, far_level = level_of(near), level_of(far)
    near_out[...] = near + middle * near_level + far_tap * far_level
    far_out[...] = far + middle * far_level + near_tap * near_level
    (halo,) = attend(features, [[a_ref, b_ref, c_ref, d_ref]], scale, scratch)
    halo = level_of(dot(halo, in_ref[:channels, :]) + base_ref[...])
    far_out[...] += jnp.where(inside, far_tap, 0.0) * halo


def mix(stream, ups, downs, hidden_ref):
    gated = (stream * inverse_rms(stream, 1e-5)).astype(BF16)
    base = 0
    total = None
    for up_ref, down_ref in zip(ups, downs):
        units = up_ref.shape[2]
        step = min(256, units)
        for at in range(0, units, step):
            x = dot(gated, up_ref[0, :, at : at + step])
            inner = x * (x * x * (0.044715 * math.sqrt(2 / math.pi)) + math.sqrt(2 / math.pi))
            hidden_ref[:, base + at : base + at + step] = (x + x * jnp.tanh(inner)).astype(BF16)
        base += units
    base = 0
    for up_ref, down_ref in zip(ups, downs):
        units = up_ref.shape[2]
        part = dot(hidden_ref[:, base : base + units], down_ref[0])
        total = part if total is None else total + part
        base += units
    return stream + 0.5 * total


def mix_far_body(own_ref, up_a, up_b, down_a, down_b, out_ref, hidden_ref):
    out_ref[...] = mix(own_ref[...], (up_a, up_b), (down_a, down_b), hidden_ref)


def mix_near_body(
    devices,
    halo_ref,
    own_ref,
    base_ref,
    in_ref,
    taps_ref,
    up_a,
    up_b,
    down_a,
    down_b,
    far_ref,
    out_ref,
    hidden_ref,
    line_ref,
):
    channels = halo_ref.shape[1]
    place = lax.axis_index("frame")
    even = is_even()
    inside = jnp.logical_not(even) | (place < devices - 1)
    tap, _, _ = taps_of(taps_ref)
    halo = level_of(dot(halo_ref[...], in_ref[:channels, :]) + base_ref[...])
    stream = own_ref[...] + jnp.where(inside, tap, 0.0) * halo
    near = mix(stream, (up_a, up_b), (down_a, down_b), hidden_ref)
    far = far_ref[...]
    rows, width = far.shape
    blocks = width // LANES
    for t, value in ((0, jnp.where(even, far, near)), (1, jnp.where(even, near, far))):
        for b in range(blocks):
            line_ref[pl.ds(b * 2 + t, rows, stride=blocks * 2), :] = value[
                :, b * LANES : (b + 1) * LANES
            ]
    out_ref[...] = line_ref[...].astype(BF16)


def copy_lines(source_ref, target_ref, first, sems):
    rows = source_ref.shape[0]
    count = sems.shape[0]
    size = rows // count
    copies = [
        pltpu.make_async_copy(
            source_ref.at[pl.ds(k * size, size)],
            target_ref.at[pl.ds(first + k * size, size)],
            sems.at[k],
        )
        for k in range(count)
    ]
    for copy in copies:
        copy.start()
    for copy in copies:
        copy.wait()


def place_body(own_ref, out_ref, sems):
    copy_lines(own_ref, out_ref, lax.axis_index("split") * own_ref.shape[0], sems)


def merge_body(other_ref, _, out_ref, sems):
    copy_lines(other_ref, out_ref, (1 - lax.axis_index("split")) * other_ref.shape[0], sems)


def on_device(frames, query_frame, query_pixel, in_weight, conv_weight, up_weight, down_weight):
    frame_count, pixel_count, channels = frames.shape
    query_count = query_frame.shape[0]
    width = in_weight.shape[1]
    units = up_weight.shape[2]
    parts = lax.axis_size("split")
    devices = lax.axis_size("frame")
    assert parts == 2 and frame_count == 2 and devices > 1 and devices & (devices - 1) == 0
    rows = query_count // parts
    swap = [(0, 1), (1, 0)]
    flips = lambda mask: [(i, i ^ mask) for i in range(devices)]
    mine, frames, outer = call(
        functools.partial(pick_body, parts),
        (
            kept((rows, channels), BF16),
            kept(frames.shape, BF16),
            kept((pixel_count // parts // 2, channels), BF16),
        ),
        3,
        scratch=(
            pltpu.VMEM((1, query_count), jnp.int32),
            pltpu.VMEM(query_pixel.shape, jnp.int32),
            pltpu.SemaphoreType.DMA((3 + frame_count * pixel_count // min(512, pixel_count),)),
        ),
        in_specs=[HBM] * 3,
    )(*(fixed(x) for x in (query_frame.reshape(1, query_count), query_pixel, frames)))
    pairs = [
        (parts * i + c, parts * (i + 1) + c) for i in range(1, devices - 1, 2) for c in range(parts)
    ] + [(parts * i, parts * i + 1) for i in (0, devices - 1)]
    masks = [2 * (1 << k) - 1 for k in range(devices.bit_length() - 1)]
    theirs = lax.ppermute(mine, "frame", flips(masks[0]))
    outer = lax.ppermute(outer, ("frame", "split"), pairs + [(b, a) for a, b in pairs])
    up_other = lax.ppermute(up_weight, "split", swap)
    down_other = lax.ppermute(down_weight, "split", swap)
    theirs, up_other, down_other = held(theirs), held(up_other), held(down_other)
    outer = held(outer)
    for mask in masks[1:]:
        mine = call(join_body, kept((rows, channels), BF16), 2)(mine, theirs)
        theirs = lax.ppermute(mine, "frame", flips(mask))
        theirs = held(theirs)
    groups = lax.axis_size("query")
    assert groups % 2 == 0
    outer_b = lax.ppermute(outer, "query", [(g, g ^ 1) for g in range(groups)])
    outer_b = held(outer_b)
    outer_c = lax.ppermute(outer, "split", swap)
    outer_d = lax.ppermute(outer_b, "split", swap)
    outers = (outer, outer_b, held(outer_c), held(outer_d))
    in_weight = held(in_weight)
    taps = held(conv_weight.reshape(1, conv_weight.shape[1] * width))
    weights = (held(up_weight), up_other, held(down_weight), down_other)
    scale = math.log2(math.e) / math.sqrt(channels)
    attention = lambda count: (
        pltpu.VMEM((count, rows, pixel_count), F32),
        pltpu.VMEM((count, rows, pixel_count), BF16),
        pltpu.VMEM((count, rows, LANES), F32),
    )
    small = kept((rows, channels), BF16)
    wide = kept((rows, width), F32)
    features, near = call(
        functools.partial(near_body, scale), (small, small), 3, attention(1)
    )(mine, theirs, frames)
    near_halo = lax.ppermute(near, "frame", flips(1))
    near_halo = held(near_halo)
    far = call(functools.partial(far_body, scale), small, 2, attention(1))(features, frames)
    base, own_near, own_far = call(
        functools.partial(own_body, devices, scale), (wide,) * 3, 9, attention(1)
    )(features, near, far, *outers, in_weight, taps)
    hidden = pltpu.VMEM((rows, parts * units), BF16)
    far = call(mix_far_body, wide, 5, (hidden,))(own_far, *weights)
    blocks = width // LANES
    lines = rows * blocks * frame_count
    own = call(
        functools.partial(mix_near_body, devices),
        kept((lines, LANES), BF16),
        10,
        (hidden, pltpu.VMEM((lines, LANES), F32)),
    )(near_halo, own_near, base, in_weight, taps, *weights, far)
    other = held(lax.ppermute(own, "split", swap))
    whole = jax.ShapeDtypeStruct((parts * lines, LANES), BF16)
    moves = (pltpu.SemaphoreType.DMA((4,)),)
    both = call(place_body, whole, 1, moves, out_specs=HBM)(own)
    both = call(
        merge_body, whole, 2, moves, in_specs=[VMEM, HBM], out_specs=HBM, aliases={1: 0}
    )(other, both)
    both = both.reshape(query_count, blocks, frame_count, LANES)
    return both.transpose(0, 2, 1, 3).reshape(query_count, frame_count, width)


def solution(mesh):
    return jax.shard_map(
        on_device,
        mesh=mesh,
        in_specs=(
            P(("dom", "frame"), None, None),
            P(("dom", "query")),
            P(None, ("dom", "query")),
            P(),
            P(),
            P(None, None, "split"),
            P(None, "split", None),
        ),
        out_specs=P(("dom", "query"), "frame", None),
        check_vma=False,
    )
```

```python
import functools
import math

import jax
import jax.numpy as jnp
from jax import lax
from jax.experimental import pallas as pl
from jax.experimental.pallas import tpu as pltpu
from jax.sharding import PartitionSpec as P


LANES = 128
ROOM = 20 * 1024 * 1024
BF16 = jnp.bfloat16
F32 = jnp.float32
VMEM = pl.BlockSpec(memory_space=pltpu.VMEM)
HBM = pl.BlockSpec(memory_space=pltpu.HBM)


def held(value):
    return pltpu.with_memory_space_constraint(value, pltpu.VMEM)


def fixed(value):
    return pltpu.with_memory_space_constraint(value, pltpu.HBM)


def kept(shape, dtype):
    return pltpu.VMEM(shape, dtype)


def call(body, out, count, scratch=(), in_specs=None, out_specs=None, aliases=None):
    many = isinstance(out, tuple)
    if out_specs is None:
        out_specs = (VMEM,) * len(out) if many else VMEM
    return pl.pallas_call(
        body,
        out_shape=out,
        in_specs=[VMEM] * count if in_specs is None else in_specs,
        out_specs=out_specs,
        scratch_shapes=list(scratch),
        input_output_aliases=aliases or {},
        compiler_params=pltpu.CompilerParams(vmem_limit_bytes=ROOM),
    )


def dot(a, b):
    return jnp.dot(a, b, preferred_element_type=F32)


def dot_t(a, b):
    return lax.dot_general(a, b, (((1,), (1,)), ((), ())), preferred_element_type=F32)


def my_part(whole, part, parts):
    size = whole.shape[-1] // parts
    mine = whole[:, :size]
    for at in range(1, parts):
        mine = jnp.where(part == at, whole[:, at * size : (at + 1) * size], mine)
    return mine


def is_even():
    return lax.rem(lax.axis_index("frame"), 2) == 0


def near_frame():
    return 1 - lax.rem(lax.axis_index("frame"), 2)


def inverse_rms(values, epsilon):
    return lax.rsqrt(jnp.mean(values * values, axis=-1, keepdims=True) + epsilon)


def level_of(stream):
    return (stream * inverse_rms(stream, 1e-5)).astype(BF16).astype(F32)


def pick_body(
    parts,
    frame_hbm,
    pixel_hbm,
    frames_hbm,
    out_ref,
    frames_ref,
    outer_ref,
    frame_ref,
    pixel_ref,
    sems,
):
    frame_count, pixel_count, _ = frames_ref.shape
    loads = [
        pltpu.make_async_copy(frame_hbm, frame_ref, sems.at[0]),
        pltpu.make_async_copy(pixel_hbm, pixel_ref, sems.at[1]),
    ]
    chunk = min(512, pixel_count)
    spots = [(at, t) for at in range(0, pixel_count, chunk) for t in range(frame_count)]
    maps = [
        pltpu.make_async_copy(
            frames_hbm.at[t, pl.ds(at, chunk)], frames_ref.at[t, pl.ds(at, chunk)], sems.at[2 + k]
        )
        for k, (at, t) in enumerate(spots)
    ]
    part = lax.axis_index("split")
    share = outer_ref.shape[0]
    side_of_pair = lax.rem(lax.axis_index("query"), 2)
    outer = pltpu.make_async_copy(
        frames_hbm.at[1 - near_frame(), pl.ds((2 * part + side_of_pair) * share, share)], outer_ref, sems.at[2 + len(maps)]
    )
    for copy in loads + maps + [outer]:
        copy.start()
    for copy in loads:
        copy.wait()
    first = lax.axis_index("frame") * frame_count
    side = math.isqrt(pixel_count)
    pixel = pixel_ref[...]
    local = my_part(frame_ref[...], part, parts) - first
    row = my_part(pixel[0:1], part, parts)
    col = my_part(pixel[1:2], part, parts)
    place = row * side + col
    count = place.shape[1]
    line = lax.broadcasted_iota(jnp.int32, (8, count), 0)
    both = jnp.transpose(jnp.where(line == 0, place, local))
    place = jnp.broadcast_to(both[:, :1], (count, LANES))
    local = jnp.broadcast_to(both[:, 1:2], (count, LANES))
    order = lax.broadcasted_iota(jnp.int32, (count, LANES), 1)
    totals = [None] * frame_count
    for at in range(0, pixel_count, chunk):
        hot = jnp.concatenate(
            [
                jnp.where(place == order + k, 1.0, 0.0).astype(BF16)
                for k in range(at, at + chunk, LANES)
            ],
            axis=1,
        )
        for t in range(frame_count):
            maps[spots.index((at, t))].wait()
        for t in range(frame_count):
            part_sum = dot(hot, frames_ref[t, at : at + chunk, :])
            totals[t] = part_sum if at == 0 else totals[t] + part_sum
    for b in range(0, out_ref.shape[1], LANES):
        picked = jnp.zeros((count, LANES), F32)
        for t in range(frame_count):
            picked = jnp.where(local == t, totals[t][:, b : b + LANES], picked)
        out_ref[:, b : b + LANES] = picked.astype(BF16)
    outer.wait()


def join_body(a_ref, b_ref, out_ref):
    out_ref[...] = a_ref[...] + b_ref[...]


def attend(features, maps, scale, scratch):
    score_ref, weight_ref, sum_ref = scratch
    rows = features.shape[0]
    step = 32
    for k, blocks in enumerate(maps):
        at = 0
        for block in blocks:
            score_ref[k, :, at : at + block.shape[0]] = dot_t(features, block[...])
            at += block.shape[0]
    for k in range(len(maps)):
        for at in range(0, rows, step):
            scores = score_ref[k, at : at + step, :]
            peak = jnp.max(scores, axis=-1, keepdims=True)
            expd = jnp.exp2((scores - peak) * scale)
            total = jnp.sum(expd, axis=-1, keepdims=True)
            sum_ref[k, at : at + step, :] = jnp.broadcast_to(total, (step, LANES))
            weight_ref[k, at : at + step, :] = expd.astype(BF16)
    out = []
    for k, blocks in enumerate(maps):
        at = 0
        pooled = None
        for block in blocks:
            part = dot(weight_ref[k, :, at : at + block.shape[0]], block[...])
            pooled = part if pooled is None else pooled + part
            at += block.shape[0]
        total = sum_ref[k, :, :1]
        mean = jnp.mean(pooled * pooled, axis=-1, keepdims=True)
        out.append((pooled * lax.rsqrt(mean + 1e-6 * total * total)).astype(BF16))
    return out


def near_body(scale, a_ref, b_ref, frames_ref, features_ref, normed_ref, *scratch):
    features = a_ref[...] + b_ref[...]
    features_ref[...] = features
    (normed_ref[...],) = attend(features, [[frames_ref.at[near_frame()]]], scale, scratch)


def far_body(scale, features_ref, frames_ref, normed_ref, *scratch):
    maps = [[frames_ref.at[1 - near_frame()]]]
    (normed_ref[...],) = attend(features_ref[...], maps, scale, scratch)


def taps_of(taps_ref):
    width = taps_ref.shape[1] // 3
    first, middle, last = (taps_ref[:, k * width : (k + 1) * width] for k in range(3))
    even = is_even()
    return jnp.where(even, last, first), middle, jnp.where(even, first, last)


def own_body(
    devices,
    scale,
    features_ref,
    near_ref,
    far_ref,
    a_ref,
    b_ref,
    c_ref,
    d_ref,
    in_ref,
    taps_ref,
    base_ref,
    near_out,
    far_out,
    *scratch,
):
    features = features_ref[...]
    channels = features.shape[1]
    near_tap, middle, far_tap = taps_of(taps_ref)
    place = lax.axis_index("frame")
    inside = jnp.where(is_even(), place > 0, place < devices - 1)
    base = dot(features, in_ref[channels:, :])
    base_ref[...] = base
    near = dot(near_ref[...], in_ref[:channels, :]) + base
    far = dot(far_ref[...], in_ref[:channels, :]) + base
    near_level, far_level = level_of(near), level_of(far)
    near_out[...] = near + middle * near_level + far_tap * far_level
    far_out[...] = far + middle * far_level + near_tap * near_level
    (halo,) = attend(features, [[a_ref, b_ref, c_ref, d_ref]], scale, scratch)
    halo = level_of(dot(halo, in_ref[:channels, :]) + base_ref[...])
    far_out[...] += jnp.where(inside, far_tap, 0.0) * halo


def mix(stream, ups, downs, hidden_ref):
    gated = (stream * inverse_rms(stream, 1e-5)).astype(BF16)
    base = 0
    total = None
    for up_ref, down_ref in zip(ups, downs):
        units = up_ref.shape[2]
        step = min(256, units)
        for at in range(0, units, step):
            x = dot(gated, up_ref[0, :, at : at + step])
            inner = x * (x * x * (0.044715 * math.sqrt(2 / math.pi)) + math.sqrt(2 / math.pi))
            hidden_ref[:, base + at : base + at + step] = (x + x * jnp.tanh(inner)).astype(BF16)
        base += units
    base = 0
    for up_ref, down_ref in zip(ups, downs):
        units = up_ref.shape[2]
        part = dot(hidden_ref[:, base : base + units], down_ref[0])
        total = part if total is None else total + part
        base += units
    return stream + 0.5 * total


def mix_far_body(own_ref, up_a, up_b, down_a, down_b, out_ref, hidden_ref):
    out_ref[...] = mix(own_ref[...], (up_a, up_b), (down_a, down_b), hidden_ref)


def mix_near_body(
    devices,
    halo_ref,
    own_ref,
    base_ref,
    in_ref,
    taps_ref,
    up_a,
    up_b,
    down_a,
    down_b,
    far_ref,
    out_ref,
    hidden_ref,
    line_ref,
):
    channels = halo_ref.shape[1]
    place = lax.axis_index("frame")
    even = is_even()
    inside = jnp.logical_not(even) | (place < devices - 1)
    tap, _, _ = taps_of(taps_ref)
    halo = level_of(dot(halo_ref[...], in_ref[:channels, :]) + base_ref[...])
    stream = own_ref[...] + jnp.where(inside, tap, 0.0) * halo
    near = mix(stream, (up_a, up_b), (down_a, down_b), hidden_ref)
    far = far_ref[...]
    rows, width = far.shape
    blocks = width // LANES
    for t, value in ((0, jnp.where(even, far, near)), (1, jnp.where(even, near, far))):
        for b in range(blocks):
            line_ref[pl.ds(b * 2 + t, rows, stride=blocks * 2), :] = value[
                :, b * LANES : (b + 1) * LANES
            ]
    out_ref[...] = line_ref[...].astype(BF16)


def copy_lines(source_ref, target_ref, first, sems):
    rows = source_ref.shape[0]
    count = sems.shape[0]
    size = rows // count
    copies = [
        pltpu.make_async_copy(
            source_ref.at[pl.ds(k * size, size)],
            target_ref.at[pl.ds(first + k * size, size)],
            sems.at[k],
        )
        for k in range(count)
    ]
    for copy in copies:
        copy.start()
    for copy in copies:
        copy.wait()


def place_body(own_ref, out_ref, sems):
    copy_lines(own_ref, out_ref, lax.axis_index("split") * own_ref.shape[0], sems)


def merge_body(other_ref, _, out_ref, sems):
    copy_lines(other_ref, out_ref, (1 - lax.axis_index("split")) * other_ref.shape[0], sems)


def on_device(frames, query_frame, query_pixel, in_weight, conv_weight, up_weight, down_weight):
    frame_count, pixel_count, channels = frames.shape
    query_count = query_frame.shape[0]
    width = in_weight.shape[1]
    units = up_weight.shape[2]
    parts = lax.axis_size("split")
    devices = lax.axis_size("frame")
    assert parts == 2 and frame_count == 2 and devices > 1 and devices & (devices - 1) == 0
    rows = query_count // parts
    swap = [(0, 1), (1, 0)]
    flips = lambda mask: [(i, i ^ mask) for i in range(devices)]
    mine, frames, outer = call(
        functools.partial(pick_body, parts),
        (
            kept((rows, channels), BF16),
            kept(frames.shape, BF16),
            kept((pixel_count // parts // 2, channels), BF16),
        ),
        3,
        scratch=(
            pltpu.VMEM((1, query_count), jnp.int32),
            pltpu.VMEM(query_pixel.shape, jnp.int32),
            pltpu.SemaphoreType.DMA((3 + frame_count * pixel_count // min(512, pixel_count),)),
        ),
        in_specs=[HBM] * 3,
    )(*(fixed(x) for x in (query_frame.reshape(1, query_count), query_pixel, frames)))
    pairs = [
        (parts * i + c, parts * (i + 1) + c) for i in range(1, devices - 1, 2) for c in range(parts)
    ] + [(parts * i, parts * i + 1) for i in (0, devices - 1)]
    masks = [2 * (1 << k) - 1 for k in range(devices.bit_length() - 1)]
    theirs = lax.ppermute(mine, "frame", flips(masks[0]))
    outer = lax.ppermute(outer, ("frame", "split"), pairs + [(b, a) for a, b in pairs])
    up_other = lax.ppermute(up_weight, "split", swap)
    down_other = lax.ppermute(down_weight, "split", swap)
    theirs, up_other, down_other = held(theirs), held(up_other), held(down_other)
    outer = held(outer)
    for mask in masks[1:]:
        mine = call(join_body, kept((rows, channels), BF16), 2)(mine, theirs)
        theirs = lax.ppermute(mine, "frame", flips(mask))
        theirs = held(theirs)
    groups = lax.axis_size("query")
    assert groups % 2 == 0
    outer_b = lax.ppermute(outer, "query", [(g, g ^ 1) for g in range(groups)])
    outer_b = held(outer_b)
    outer_c = lax.ppermute(outer, "split", swap)
    outer_d = lax.ppermute(outer_b, "split", swap)
    outers = (outer, outer_b, held(outer_c), held(outer_d))
    in_weight = held(in_weight)
    taps = held(conv_weight.reshape(1, conv_weight.shape[1] * width))
    weights = (held(up_weight), up_other, held(down_weight), down_other)
    scale = math.log2(math.e) / math.sqrt(channels)
    attention = lambda count: (
        pltpu.VMEM((count, rows, pixel_count), F32),
        pltpu.VMEM((count, rows, pixel_count), BF16),
        pltpu.VMEM((count, rows, LANES), F32),
    )
    small = kept((rows, channels), BF16)
    wide = kept((rows, width), F32)
    features, near = call(
        functools.partial(near_body, scale), (small, small), 3, attention(1)
    )(mine, theirs, frames)
    near_halo = lax.ppermute(near, "frame", flips(1))
    near_halo = held(near_halo)
    far = call(functools.partial(far_body, scale), small, 2, attention(1))(features, frames)
    base, own_near, own_far = call(
        functools.partial(own_body, devices, scale), (wide,) * 3, 9, attention(1)
    )(features, near, far, *outers, in_weight, taps)
    hidden = pltpu.VMEM((rows, parts * units), BF16)
    far = call(mix_far_body, wide, 5, (hidden,))(own_far, *weights)
    blocks = width // LANES
    lines = rows * blocks * frame_count
    own = call(
        functools.partial(mix_near_body, devices),
        kept((lines, LANES), BF16),
        10,
        (hidden, pltpu.VMEM((lines, LANES), F32)),
    )(near_halo, own_near, base, in_weight, taps, *weights, far)
    other = held(lax.ppermute(own, "split", swap))
    whole = jax.ShapeDtypeStruct((parts * lines, LANES), BF16)
    moves = (pltpu.SemaphoreType.DMA((4,)),)
    both = call(place_body, whole, 1, moves, out_specs=HBM)(own)
    both = call(
        merge_body, whole, 2, moves, in_specs=[VMEM, HBM], out_specs=HBM, aliases={1: 0}
    )(other, both)
    both = both.reshape(query_count, blocks, frame_count, LANES)
    return both.transpose(0, 2, 1, 3).reshape(query_count, frame_count, width)


def solution(mesh):
    return jax.shard_map(
        on_device,
        mesh=mesh,
        in_specs=(
            P(("dom", "frame"), None, None),
            P(("dom", "query")),
            P(None, ("dom", "query")),
            P(),
            P(),
            P(None, None, "split"),
            P(None, "split", None),
        ),
        out_specs=P(("dom", "query"), "frame", None),
        check_vma=False,
    )
```

```python
import functools
import math

import jax
import jax.numpy as jnp
from jax import lax
from jax.experimental import pallas as pl
from jax.experimental.pallas import tpu as pltpu
from jax.sharding import PartitionSpec as P


LANES = 128
ROOM = 20 * 1024 * 1024
BF16 = jnp.bfloat16
F32 = jnp.float32
VMEM = pl.BlockSpec(memory_space=pltpu.VMEM)
HBM = pl.BlockSpec(memory_space=pltpu.HBM)


def held(value):
    return pltpu.with_memory_space_constraint(value, pltpu.VMEM)


def fixed(value):
    return pltpu.with_memory_space_constraint(value, pltpu.HBM)


def kept(shape, dtype):
    return pltpu.VMEM(shape, dtype)


def call(body, out, count, scratch=(), in_specs=None, out_specs=None, aliases=None):
    many = isinstance(out, tuple)
    if out_specs is None:
        out_specs = (VMEM,) * len(out) if many else VMEM
    return pl.pallas_call(
        body,
        out_shape=out,
        in_specs=[VMEM] * count if in_specs is None else in_specs,
        out_specs=out_specs,
        scratch_shapes=list(scratch),
        input_output_aliases=aliases or {},
        compiler_params=pltpu.CompilerParams(vmem_limit_bytes=ROOM),
    )


def dot(a, b):
    return jnp.dot(a, b, preferred_element_type=F32)


def my_part(whole, part, parts):
    size = whole.shape[-1] // parts
    mine = whole[:, :size]
    for at in range(1, parts):
        mine = jnp.where(part == at, whole[:, at * size : (at + 1) * size], mine)
    return mine


def is_even():
    return lax.rem(lax.axis_index("frame"), 2) == 0


def near_frame():
    return 1 - lax.rem(lax.axis_index("frame"), 2)


def inverse_rms(values, epsilon):
    return lax.rsqrt(jnp.mean(values * values, axis=-1, keepdims=True) + epsilon)


def level_of(stream):
    return (stream * inverse_rms(stream, 1e-5)).astype(BF16).astype(F32)


def pick_body(
    parts,
    frame_hbm,
    pixel_hbm,
    frames_hbm,
    out_ref,
    frames_ref,
    outer_ref,
    frame_ref,
    pixel_ref,
    sems,
):
    frame_count, pixel_count, _ = frames_ref.shape
    loads = [
        pltpu.make_async_copy(frame_hbm, frame_ref, sems.at[0]),
        pltpu.make_async_copy(pixel_hbm, pixel_ref, sems.at[1]),
    ]
    chunk = min(512, pixel_count)
    spots = [(at, t) for at in range(0, pixel_count, chunk) for t in range(frame_count)]
    maps = [
        pltpu.make_async_copy(
            frames_hbm.at[t, pl.ds(at, chunk)], frames_ref.at[t, pl.ds(at, chunk)], sems.at[2 + k]
        )
        for k, (at, t) in enumerate(spots)
    ]
    part = lax.axis_index("split")
    share = outer_ref.shape[0]
    side_of_pair = lax.rem(lax.axis_index("query"), 2)
    outer = pltpu.make_async_copy(
        frames_hbm.at[1 - near_frame(), pl.ds((2 * part + side_of_pair) * share, share)], outer_ref, sems.at[2 + len(maps)]
    )
    for copy in loads + maps + [outer]:
        copy.start()
    for copy in loads:
        copy.wait()
    first = lax.axis_index("frame") * frame_count
    side = math.isqrt(pixel_count)
    pixel = pixel_ref[...]
    local = my_part(frame_ref[...], part, parts) - first
    row = my_part(pixel[0:1], part, parts)
    col = my_part(pixel[1:2], part, parts)
    place = row * side + col
    count = place.shape[1]
    line = lax.broadcasted_iota(jnp.int32, (8, count), 0)
    both = jnp.transpose(jnp.where(line == 0, place, local))
    place = jnp.broadcast_to(both[:, :1], (count, LANES))
    local = jnp.broadcast_to(both[:, 1:2], (count, LANES))
    order = lax.broadcasted_iota(jnp.int32, (count, LANES), 1)
    totals = [None] * frame_count
    for at in range(0, pixel_count, chunk):
        hot = jnp.concatenate(
            [
                jnp.where(place == order + k, 1.0, 0.0).astype(BF16)
                for k in range(at, at + chunk, LANES)
            ],
            axis=1,
        )
        for t in range(frame_count):
            maps[spots.index((at, t))].wait()
        for t in range(frame_count):
            part_sum = dot(hot, frames_ref[t, at : at + chunk, :])
            totals[t] = part_sum if at == 0 else totals[t] + part_sum
    for b in range(0, out_ref.shape[1], LANES):
        picked = jnp.zeros((count, LANES), F32)
        for t in range(frame_count):
            picked = jnp.where(local == t, totals[t][:, b : b + LANES], picked)
        out_ref[:, b : b + LANES] = picked.astype(BF16)
    outer.wait()


def join_body(a_ref, b_ref, out_ref):
    out_ref[...] = a_ref[...] + b_ref[...]


def attend_split(features, blocks, scale, scratch):
    rows, size = features.shape
    sums = [pltpu.ACC(k % 2)((rows, size), F32) for k in range(len(blocks))]
    return pl.run_scoped(functools.partial(attend_units, features, blocks, scale, scratch), *sums)


def attend_units(features, blocks, scale, scratch, *sums):
    score_ref, weight_ref, sum_ref = scratch
    rows, size = features.shape
    step = 32
    for j, block in enumerate(blocks):
        unit, slot = j % 2, j // 2
        at = j * size
        acc = sums[j]
        pltpu.matmul_push_rhs(block[...], slot % 2, unit, transpose=True)
        pltpu.matmul_acc_lhs(acc, features, load_staged_rhs=slot % 2)
        score_ref[0, :, at : at + size] = pltpu.matmul_pop(acc)
    for at in range(0, rows, step):
        scores = score_ref[0, at : at + step, :]
        peak = jnp.max(scores, axis=-1, keepdims=True)
        expd = jnp.exp2((scores - peak) * scale)
        total = jnp.sum(expd, axis=-1, keepdims=True)
        sum_ref[0, at : at + step, :] = jnp.broadcast_to(total, (step, LANES))
        weight_ref[0, at : at + step, :] = expd.astype(BF16)
    for j, block in enumerate(blocks):
        unit, slot = j % 2, j // 2
        at = j * size
        pltpu.matmul_push_rhs(block[...], slot % 2, unit)
        pltpu.matmul_acc_lhs(
            sums[unit], weight_ref[0, :, at : at + size], load_staged_rhs=slot % 2
        )
    pooled = pltpu.matmul_pop(sums[0]) + pltpu.matmul_pop(sums[1])
    total = sum_ref[0, :, :1]
    mean = jnp.mean(pooled * pooled, axis=-1, keepdims=True)
    return (pooled * lax.rsqrt(mean + 1e-6 * total * total)).astype(BF16)


def blocks_of(frames_ref, t):
    size = frames_ref.shape[2]
    return [frames_ref.at[t, pl.ds(at, size)] for at in range(0, frames_ref.shape[1], size)]


def near_body(scale, a_ref, b_ref, frames_ref, features_ref, normed_ref, *scratch):
    features = a_ref[...] + b_ref[...]
    features_ref[...] = features
    normed_ref[...] = attend_split(features, blocks_of(frames_ref, near_frame()), scale, scratch)


def far_body(scale, features_ref, frames_ref, normed_ref, *scratch):
    blocks = blocks_of(frames_ref, 1 - near_frame())
    normed_ref[...] = attend_split(features_ref[...], blocks, scale, scratch)


def halo_body(scale, features_ref, a_ref, b_ref, c_ref, d_ref, normed_ref, *scratch):
    blocks = [a_ref, b_ref, c_ref, d_ref]
    normed_ref[...] = attend_split(features_ref[...], blocks, scale, scratch)


def taps_of(taps_ref):
    width = taps_ref.shape[1] // 3
    first, middle, last = (taps_ref[:, k * width : (k + 1) * width] for k in range(3))
    even = is_even()
    return jnp.where(even, last, first), middle, jnp.where(even, first, last)


def own_body(features_ref, near_ref, far_ref, in_ref, taps_ref, base_ref, near_out, far_out):
    channels = features_ref.shape[1]
    near_tap, middle, far_tap = taps_of(taps_ref)
    base = dot(features_ref[...], in_ref[channels:, :])
    base_ref[...] = base
    near = dot(near_ref[...], in_ref[:channels, :]) + base
    far = dot(far_ref[...], in_ref[:channels, :]) + base
    near_level, far_level = level_of(near), level_of(far)
    near_out[...] = near + middle * near_level + far_tap * far_level
    far_out[...] = far + middle * far_level + near_tap * near_level


def with_halo(halo_ref, own_ref, base_ref, in_ref, tap, inside):
    channels = halo_ref.shape[1]
    halo = level_of(dot(halo_ref[...], in_ref[:channels, :]) + base_ref[...])
    return own_ref[...] + jnp.where(inside, tap, 0.0) * halo


def mix(stream, ups, downs, hidden_ref):
    gated = (stream * inverse_rms(stream, 1e-5)).astype(BF16)
    base = 0
    total = None
    for up_ref, down_ref in zip(ups, downs):
        units = up_ref.shape[2]
        step = min(256, units)
        for at in range(0, units, step):
            x = dot(gated, up_ref[0, :, at : at + step])
            inner = x * (x * x * (0.044715 * math.sqrt(2 / math.pi)) + math.sqrt(2 / math.pi))
            hidden_ref[:, base + at : base + at + step] = (x + x * jnp.tanh(inner)).astype(BF16)
        base += units
    base = 0
    for up_ref, down_ref in zip(ups, downs):
        units = up_ref.shape[2]
        part = dot(hidden_ref[:, base : base + units], down_ref[0])
        total = part if total is None else total + part
        base += units
    return stream + 0.5 * total


def mix_far_body(
    devices, halo_ref, own_ref, base_ref, in_ref, taps_ref, up_a, up_b, down_a, down_b, out_ref, hidden_ref
):
    place = lax.axis_index("frame")
    inside = jnp.where(is_even(), place > 0, place < devices - 1)
    _, _, tap = taps_of(taps_ref)
    stream = with_halo(halo_ref, own_ref, base_ref, in_ref, tap, inside)
    out_ref[...] = mix(stream, (up_a, up_b), (down_a, down_b), hidden_ref)


def mix_near_body(
    devices,
    halo_ref,
    own_ref,
    base_ref,
    in_ref,
    taps_ref,
    up_a,
    up_b,
    down_a,
    down_b,
    far_ref,
    out_ref,
    hidden_ref,
    line_ref,
):
    place = lax.axis_index("frame")
    even = is_even()
    inside = jnp.logical_not(even) | (place < devices - 1)
    tap, _, _ = taps_of(taps_ref)
    stream = with_halo(halo_ref, own_ref, base_ref, in_ref, tap, inside)
    near = mix(stream, (up_a, up_b), (down_a, down_b), hidden_ref)
    far = far_ref[...]
    rows, width = far.shape
    blocks = width // LANES
    for t, value in ((0, jnp.where(even, far, near)), (1, jnp.where(even, near, far))):
        for b in range(blocks):
            line_ref[pl.ds(b * 2 + t, rows, stride=blocks * 2), :] = value[
                :, b * LANES : (b + 1) * LANES
            ]
    out_ref[...] = line_ref[...].astype(BF16)


def copy_lines(source_ref, target_ref, first, sems):
    rows = source_ref.shape[0]
    count = sems.shape[0]
    size = rows // count
    copies = [
        pltpu.make_async_copy(
            source_ref.at[pl.ds(k * size, size)],
            target_ref.at[pl.ds(first + k * size, size)],
            sems.at[k],
        )
        for k in range(count)
    ]
    for copy in copies:
        copy.start()
    for copy in copies:
        copy.wait()


def place_body(own_ref, out_ref, sems):
    copy_lines(own_ref, out_ref, lax.axis_index("split") * own_ref.shape[0], sems)


def merge_body(other_ref, _, out_ref, sems):
    copy_lines(other_ref, out_ref, (1 - lax.axis_index("split")) * other_ref.shape[0], sems)


def on_device(frames, query_frame, query_pixel, in_weight, conv_weight, up_weight, down_weight):
    frame_count, pixel_count, channels = frames.shape
    query_count = query_frame.shape[0]
    width = in_weight.shape[1]
    units = up_weight.shape[2]
    parts = lax.axis_size("split")
    devices = lax.axis_size("frame")
    assert parts == 2 and frame_count == 2 and devices > 1 and devices & (devices - 1) == 0
    rows = query_count // parts
    swap = [(0, 1), (1, 0)]
    flips = lambda mask: [(i, i ^ mask) for i in range(devices)]
    mine, frames, outer = call(
        functools.partial(pick_body, parts),
        (
            kept((rows, channels), BF16),
            kept(frames.shape, BF16),
            kept((pixel_count // parts // 2, channels), BF16),
        ),
        3,
        scratch=(
            pltpu.VMEM((1, query_count), jnp.int32),
            pltpu.VMEM(query_pixel.shape, jnp.int32),
            pltpu.SemaphoreType.DMA((3 + frame_count * pixel_count // min(512, pixel_count),)),
        ),
        in_specs=[HBM] * 3,
    )(*(fixed(x) for x in (query_frame.reshape(1, query_count), query_pixel, frames)))
    pairs = [
        (parts * i + c, parts * (i + 1) + c) for i in range(1, devices - 1, 2) for c in range(parts)
    ] + [(parts * i, parts * i + 1) for i in (0, devices - 1)]
    masks = [2 * (1 << k) - 1 for k in range(devices.bit_length() - 1)]
    theirs = lax.ppermute(mine, "frame", flips(masks[0]))
    outer = lax.ppermute(outer, ("frame", "split"), pairs + [(b, a) for a, b in pairs])
    up_other = lax.ppermute(up_weight, "split", swap)
    down_other = lax.ppermute(down_weight, "split", swap)
    theirs, up_other, down_other = held(theirs), held(up_other), held(down_other)
    outer = held(outer)
    for mask in masks[1:]:
        mine = call(join_body, kept((rows, channels), BF16), 2)(mine, theirs)
        theirs = lax.ppermute(mine, "frame", flips(mask))
        theirs = held(theirs)
    groups = lax.axis_size("query")
    assert groups % 2 == 0
    outer_b = lax.ppermute(outer, "query", [(g, g ^ 1) for g in range(groups)])
    outer_b = held(outer_b)
    outer_c = lax.ppermute(outer, "split", swap)
    outer_d = lax.ppermute(outer_b, "split", swap)
    outers = (outer, outer_b, held(outer_c), held(outer_d))
    in_weight = held(in_weight)
    taps = held(conv_weight.reshape(1, conv_weight.shape[1] * width))
    weights = (held(up_weight), up_other, held(down_weight), down_other)
    scale = math.log2(math.e) / math.sqrt(channels)
    attention = lambda count: (
        pltpu.VMEM((count, rows, pixel_count), F32),
        pltpu.VMEM((count, rows, pixel_count), BF16),
        pltpu.VMEM((count, rows, LANES), F32),
    )
    small = kept((rows, channels), BF16)
    wide = kept((rows, width), F32)
    features, near = call(
        functools.partial(near_body, scale), (small, small), 3, attention(1)
    )(mine, theirs, frames)
    near_halo = lax.ppermute(near, "frame", flips(1))
    near_halo = held(near_halo)
    far = call(functools.partial(far_body, scale), small, 2, attention(1))(features, frames)
    base, own_near, own_far = call(own_body, (wide,) * 3, 5)(features, near, far, in_weight, taps)
    far_halo = call(functools.partial(halo_body, scale), small, 5, attention(1))(features, *outers)
    hidden = pltpu.VMEM((rows, parts * units), BF16)
    far = call(functools.partial(mix_far_body, devices), wide, 9, (hidden,))(
        far_halo, own_far, base, in_weight, taps, *weights
    )
    blocks = width // LANES
    lines = rows * blocks * frame_count
    own = call(
        functools.partial(mix_near_body, devices),
        kept((lines, LANES), BF16),
        10,
        (hidden, pltpu.VMEM((lines, LANES), F32)),
    )(near_halo, own_near, base, in_weight, taps, *weights, far)
    other = held(lax.ppermute(own, "split", swap))
    whole = jax.ShapeDtypeStruct((parts * lines, LANES), BF16)
    moves = (pltpu.SemaphoreType.DMA((4,)),)
    both = call(place_body, whole, 1, moves, out_specs=HBM)(own)
    both = call(
        merge_body, whole, 2, moves, in_specs=[VMEM, HBM], out_specs=HBM, aliases={1: 0}
    )(other, both)
    both = both.reshape(query_count, blocks, frame_count, LANES)
    return both.transpose(0, 2, 1, 3).reshape(query_count, frame_count, width)


def solution(mesh):
    return jax.shard_map(
        on_device,
        mesh=mesh,
        in_specs=(
            P(("dom", "frame"), None, None),
            P(("dom", "query")),
            P(None, ("dom", "query")),
            P(),
            P(),
            P(None, None, "split"),
            P(None, "split", None),
        ),
        out_specs=P(("dom", "query"), "frame", None),
        check_vma=False,
    )
```

```python
import functools
import math

import jax
import jax.numpy as jnp
from jax import lax
from jax.experimental import pallas as pl
from jax.experimental.pallas import tpu as pltpu
from jax.sharding import PartitionSpec as P


LANES = 128
ROOM = 20 * 1024 * 1024
BF16 = jnp.bfloat16
F32 = jnp.float32
VMEM = pl.BlockSpec(memory_space=pltpu.VMEM)
HBM = pl.BlockSpec(memory_space=pltpu.HBM)


def held(value):
    return pltpu.with_memory_space_constraint(value, pltpu.VMEM)


def fixed(value):
    return pltpu.with_memory_space_constraint(value, pltpu.HBM)


def kept(shape, dtype):
    return pltpu.VMEM(shape, dtype)


def call(body, out, count, scratch=(), in_specs=None, out_specs=None, aliases=None):
    many = isinstance(out, tuple)
    if out_specs is None:
        out_specs = (VMEM,) * len(out) if many else VMEM
    return pl.pallas_call(
        body,
        out_shape=out,
        in_specs=[VMEM] * count if in_specs is None else in_specs,
        out_specs=out_specs,
        scratch_shapes=list(scratch),
        input_output_aliases=aliases or {},
        compiler_params=pltpu.CompilerParams(vmem_limit_bytes=ROOM),
    )


def dot(a, b):
    return jnp.dot(a, b, preferred_element_type=F32)


def my_part(whole, part, parts):
    size = whole.shape[-1] // parts
    mine = whole[:, :size]
    for at in range(1, parts):
        mine = jnp.where(part == at, whole[:, at * size : (at + 1) * size], mine)
    return mine


def is_even():
    return lax.rem(lax.axis_index("frame"), 2) == 0


def near_frame():
    return 1 - lax.rem(lax.axis_index("frame"), 2)


def inverse_rms(values, epsilon):
    return lax.rsqrt(jnp.mean(values * values, axis=-1, keepdims=True) + epsilon)


def level_of(stream):
    return (stream * inverse_rms(stream, 1e-5)).astype(BF16).astype(F32)


def pick_body(
    parts,
    frame_hbm,
    pixel_hbm,
    frames_hbm,
    out_ref,
    frames_ref,
    outer_ref,
    frame_ref,
    pixel_ref,
    sems,
):
    frame_count, pixel_count, _ = frames_ref.shape
    loads = [
        pltpu.make_async_copy(frame_hbm, frame_ref, sems.at[0]),
        pltpu.make_async_copy(pixel_hbm, pixel_ref, sems.at[1]),
    ]
    chunk = min(512, pixel_count)
    spots = [(at, t) for at in range(0, pixel_count, chunk) for t in range(frame_count)]
    maps = [
        pltpu.make_async_copy(
            frames_hbm.at[t, pl.ds(at, chunk)], frames_ref.at[t, pl.ds(at, chunk)], sems.at[2 + k]
        )
        for k, (at, t) in enumerate(spots)
    ]
    part = lax.axis_index("split")
    share = outer_ref.shape[0]
    side_of_pair = lax.rem(lax.axis_index("query"), 2)
    outer = pltpu.make_async_copy(
        frames_hbm.at[1 - near_frame(), pl.ds((2 * part + side_of_pair) * share, share)], outer_ref, sems.at[2 + len(maps)]
    )
    for copy in loads + maps + [outer]:
        copy.start()
    for copy in loads:
        copy.wait()
    first = lax.axis_index("frame") * frame_count
    side = math.isqrt(pixel_count)
    pixel = pixel_ref[...]
    local = my_part(frame_ref[...], part, parts) - first
    row = my_part(pixel[0:1], part, parts)
    col = my_part(pixel[1:2], part, parts)
    place = row * side + col
    count = place.shape[1]
    line = lax.broadcasted_iota(jnp.int32, (8, count), 0)
    both = jnp.transpose(jnp.where(line == 0, place, local))
    place = jnp.broadcast_to(both[:, :1], (count, LANES))
    local = jnp.broadcast_to(both[:, 1:2], (count, LANES))
    order = lax.broadcasted_iota(jnp.int32, (count, LANES), 1)
    totals = [None] * frame_count
    for at in range(0, pixel_count, chunk):
        hot = jnp.concatenate(
            [
                jnp.where(place == order + k, 1.0, 0.0).astype(BF16)
                for k in range(at, at + chunk, LANES)
            ],
            axis=1,
        )
        for t in range(frame_count):
            maps[spots.index((at, t))].wait()
        for t in range(frame_count):
            part_sum = dot(hot, frames_ref[t, at : at + chunk, :])
            totals[t] = part_sum if at == 0 else totals[t] + part_sum
    for b in range(0, out_ref.shape[1], LANES):
        picked = jnp.zeros((count, LANES), F32)
        for t in range(frame_count):
            picked = jnp.where(local == t, totals[t][:, b : b + LANES], picked)
        out_ref[:, b : b + LANES] = picked.astype(BF16)
    outer.wait()


def join_body(a_ref, b_ref, out_ref):
    out_ref[...] = a_ref[...] + b_ref[...]


def attend_split(features, blocks, scale, scratch):
    rows, size = features.shape
    sums = [pltpu.ACC(k % 2)((rows, size), F32) for k in range(len(blocks))]
    return pl.run_scoped(functools.partial(attend_units, features, blocks, scale, scratch), *sums)


def attend_units(features, blocks, scale, scratch, *sums):
    score_ref, weight_ref, sum_ref = scratch
    rows, size = features.shape
    step = 32
    for j, block in enumerate(blocks):
        unit, slot = j % 2, j // 2
        at = j * size
        acc = sums[j]
        pltpu.matmul_push_rhs(block[...], slot % 2, unit, transpose=True)
        pltpu.matmul_acc_lhs(acc, features, load_staged_rhs=slot % 2)
        score_ref[0, :, at : at + size] = pltpu.matmul_pop(acc)
    for at in range(0, rows, step):
        scores = score_ref[0, at : at + step, :]
        peak = jnp.max(scores, axis=-1, keepdims=True)
        expd = jnp.exp2((scores - peak) * scale)
        total = jnp.sum(expd, axis=-1, keepdims=True)
        sum_ref[0, at : at + step, :] = jnp.broadcast_to(total, (step, LANES))
        weight_ref[0, at : at + step, :] = expd.astype(BF16)
    for j, block in enumerate(blocks):
        unit, slot = j % 2, j // 2
        at = j * size
        pltpu.matmul_push_rhs(block[...], slot % 2, unit)
        pltpu.matmul_acc_lhs(
            sums[unit], weight_ref[0, :, at : at + size], load_staged_rhs=slot % 2
        )
    pooled = pltpu.matmul_pop(sums[0]) + pltpu.matmul_pop(sums[1])
    total = sum_ref[0, :, :1]
    mean = jnp.mean(pooled * pooled, axis=-1, keepdims=True)
    return (pooled * lax.rsqrt(mean + 1e-6 * total * total)).astype(BF16)


def blocks_of(frames_ref, t):
    size = frames_ref.shape[2]
    return [frames_ref.at[t, pl.ds(at, size)] for at in range(0, frames_ref.shape[1], size)]


def near_body(scale, a_ref, b_ref, frames_ref, features_ref, normed_ref, *scratch):
    features = a_ref[...] + b_ref[...]
    features_ref[...] = features
    normed_ref[...] = attend_split(features, blocks_of(frames_ref, near_frame()), scale, scratch)


def far_body(scale, features_ref, frames_ref, normed_ref, *scratch):
    blocks = blocks_of(frames_ref, 1 - near_frame())
    normed_ref[...] = attend_split(features_ref[...], blocks, scale, scratch)


def has_outer(devices):
    place = lax.axis_index("frame")
    return jnp.where(is_even(), place > 0, place < devices - 1)


def halo_body(devices, scale, features_ref, a_ref, b_ref, c_ref, d_ref, normed_ref, *scratch):
    inside = has_outer(devices)

    @pl.when(inside)
    def _():
        blocks = [a_ref, b_ref, c_ref, d_ref]
        normed_ref[...] = attend_split(features_ref[...], blocks, scale, scratch)

    @pl.when(jnp.logical_not(inside))
    def _():
        normed_ref[...] = jnp.zeros_like(normed_ref)


def taps_of(taps_ref):
    width = taps_ref.shape[1] // 3
    first, middle, last = (taps_ref[:, k * width : (k + 1) * width] for k in range(3))
    even = is_even()
    return jnp.where(even, last, first), middle, jnp.where(even, first, last)


def own_body(features_ref, near_ref, far_ref, in_ref, taps_ref, base_ref, near_out, far_out):
    channels = features_ref.shape[1]
    near_tap, middle, far_tap = taps_of(taps_ref)
    base = dot(features_ref[...], in_ref[channels:, :])
    base_ref[...] = base
    near = dot(near_ref[...], in_ref[:channels, :]) + base
    far = dot(far_ref[...], in_ref[:channels, :]) + base
    near_level, far_level = level_of(near), level_of(far)
    near_out[...] = near + middle * near_level + far_tap * far_level
    far_out[...] = far + middle * far_level + near_tap * near_level


def with_halo(halo_ref, own_ref, base_ref, in_ref, tap, inside):
    channels = halo_ref.shape[1]
    halo = level_of(dot(halo_ref[...], in_ref[:channels, :]) + base_ref[...])
    return own_ref[...] + jnp.where(inside, tap, 0.0) * halo


def mix(stream, ups, downs, hidden_ref):
    gated = (stream * inverse_rms(stream, 1e-5)).astype(BF16)
    base = 0
    total = None
    for up_ref, down_ref in zip(ups, downs):
        units = up_ref.shape[2]
        step = min(256, units)
        for at in range(0, units, step):
            x = dot(gated, up_ref[0, :, at : at + step])
            inner = x * (x * x * (0.044715 * math.sqrt(2 / math.pi)) + math.sqrt(2 / math.pi))
            hidden_ref[:, base + at : base + at + step] = (x + x * jnp.tanh(inner)).astype(BF16)
        base += units
    base = 0
    for up_ref, down_ref in zip(ups, downs):
        units = up_ref.shape[2]
        part = dot(hidden_ref[:, base : base + units], down_ref[0])
        total = part if total is None else total + part
        base += units
    return stream + 0.5 * total


def mix_far_body(
    devices, halo_ref, own_ref, base_ref, in_ref, taps_ref, up_a, up_b, down_a, down_b, out_ref, hidden_ref
):
    inside = has_outer(devices)
    out_ref[...] = own_ref[...]

    @pl.when(inside)
    def _():
        _, _, tap = taps_of(taps_ref)
        out_ref[...] = with_halo(halo_ref, own_ref, base_ref, in_ref, tap, inside)

    out_ref[...] = mix(out_ref[...], (up_a, up_b), (down_a, down_b), hidden_ref)


def mix_near_body(
    devices,
    halo_ref,
    own_ref,
    base_ref,
    in_ref,
    taps_ref,
    up_a,
    up_b,
    down_a,
    down_b,
    far_ref,
    out_ref,
    hidden_ref,
    line_ref,
):
    place = lax.axis_index("frame")
    even = is_even()
    inside = jnp.logical_not(even) | (place < devices - 1)
    tap, _, _ = taps_of(taps_ref)
    stream = with_halo(halo_ref, own_ref, base_ref, in_ref, tap, inside)
    near = mix(stream, (up_a, up_b), (down_a, down_b), hidden_ref)
    far = far_ref[...]
    rows, width = far.shape
    blocks = width // LANES
    for t, value in ((0, jnp.where(even, far, near)), (1, jnp.where(even, near, far))):
        for b in range(blocks):
            line_ref[pl.ds(b * 2 + t, rows, stride=blocks * 2), :] = value[
                :, b * LANES : (b + 1) * LANES
            ]
    out_ref[...] = line_ref[...].astype(BF16)


def copy_lines(source_ref, target_ref, first, sems):
    rows = source_ref.shape[0]
    count = sems.shape[0]
    size = rows // count
    copies = [
        pltpu.make_async_copy(
            source_ref.at[pl.ds(k * size, size)],
            target_ref.at[pl.ds(first + k * size, size)],
            sems.at[k],
        )
        for k in range(count)
    ]
    for copy in copies:
        copy.start()
    for copy in copies:
        copy.wait()


def place_body(own_ref, out_ref, sems):
    copy_lines(own_ref, out_ref, lax.axis_index("split") * own_ref.shape[0], sems)


def merge_body(other_ref, _, out_ref, sems):
    copy_lines(other_ref, out_ref, (1 - lax.axis_index("split")) * other_ref.shape[0], sems)


def on_device(frames, query_frame, query_pixel, in_weight, conv_weight, up_weight, down_weight):
    frame_count, pixel_count, channels = frames.shape
    query_count = query_frame.shape[0]
    width = in_weight.shape[1]
    units = up_weight.shape[2]
    parts = lax.axis_size("split")
    devices = lax.axis_size("frame")
    assert parts == 2 and frame_count == 2 and devices > 1 and devices & (devices - 1) == 0
    rows = query_count // parts
    swap = [(0, 1), (1, 0)]
    flips = lambda mask: [(i, i ^ mask) for i in range(devices)]
    mine, frames, outer = call(
        functools.partial(pick_body, parts),
        (
            kept((rows, channels), BF16),
            kept(frames.shape, BF16),
            kept((pixel_count // parts // 2, channels), BF16),
        ),
        3,
        scratch=(
            pltpu.VMEM((1, query_count), jnp.int32),
            pltpu.VMEM(query_pixel.shape, jnp.int32),
            pltpu.SemaphoreType.DMA((3 + frame_count * pixel_count // min(512, pixel_count),)),
        ),
        in_specs=[HBM] * 3,
    )(*(fixed(x) for x in (query_frame.reshape(1, query_count), query_pixel, frames)))
    pairs = [
        (parts * i + c, parts * (i + 1) + c) for i in range(1, devices - 1, 2) for c in range(parts)
    ] + [(parts * i, parts * i + 1) for i in (0, devices - 1)]
    masks = [2 * (1 << k) - 1 for k in range(devices.bit_length() - 1)]
    theirs = lax.ppermute(mine, "frame", flips(masks[0]))
    outer = lax.ppermute(outer, ("frame", "split"), pairs + [(b, a) for a, b in pairs])
    up_other = lax.ppermute(up_weight, "split", swap)
    down_other = lax.ppermute(down_weight, "split", swap)
    theirs, up_other, down_other = held(theirs), held(up_other), held(down_other)
    outer = held(outer)
    for mask in masks[1:]:
        mine = call(join_body, kept((rows, channels), BF16), 2)(mine, theirs)
        theirs = lax.ppermute(mine, "frame", flips(mask))
        theirs = held(theirs)
    groups = lax.axis_size("query")
    assert groups % 2 == 0
    outer_b = lax.ppermute(outer, "query", [(g, g ^ 1) for g in range(groups)])
    outer_b = held(outer_b)
    outer_c = lax.ppermute(outer, "split", swap)
    outer_d = lax.ppermute(outer_b, "split", swap)
    outers = (outer, outer_b, held(outer_c), held(outer_d))
    in_weight = held(in_weight)
    taps = held(conv_weight.reshape(1, conv_weight.shape[1] * width))
    weights = (held(up_weight), up_other, held(down_weight), down_other)
    scale = math.log2(math.e) / math.sqrt(channels)
    attention = lambda count: (
        pltpu.VMEM((count, rows, pixel_count), F32),
        pltpu.VMEM((count, rows, pixel_count), BF16),
        pltpu.VMEM((count, rows, LANES), F32),
    )
    small = kept((rows, channels), BF16)
    wide = kept((rows, width), F32)
    features, near = call(
        functools.partial(near_body, scale), (small, small), 3, attention(1)
    )(mine, theirs, frames)
    near_halo = lax.ppermute(near, "frame", flips(1))
    near_halo = held(near_halo)
    far = call(functools.partial(far_body, scale), small, 2, attention(1))(features, frames)
    base, own_near, own_far = call(own_body, (wide,) * 3, 5)(features, near, far, in_weight, taps)
    far_halo = call(functools.partial(halo_body, devices, scale), small, 5, attention(1))(
        features, *outers
    )
    hidden = pltpu.VMEM((rows, parts * units), BF16)
    far = call(functools.partial(mix_far_body, devices), wide, 9, (hidden,))(
        far_halo, own_far, base, in_weight, taps, *weights
    )
    blocks = width // LANES
    lines = rows * blocks * frame_count
    own = call(
        functools.partial(mix_near_body, devices),
        kept((lines, LANES), BF16),
        10,
        (hidden, pltpu.VMEM((lines, LANES), F32)),
    )(near_halo, own_near, base, in_weight, taps, *weights, far)
    other = held(lax.ppermute(own, "split", swap))
    whole = jax.ShapeDtypeStruct((parts * lines, LANES), BF16)
    moves = (pltpu.SemaphoreType.DMA((4,)),)
    both = call(place_body, whole, 1, moves, out_specs=HBM)(own)
    both = call(
        merge_body, whole, 2, moves, in_specs=[VMEM, HBM], out_specs=HBM, aliases={1: 0}
    )(other, both)
    both = both.reshape(query_count, blocks, frame_count, LANES)
    return both.transpose(0, 2, 1, 3).reshape(query_count, frame_count, width)


def solution(mesh):
    return jax.shard_map(
        on_device,
        mesh=mesh,
        in_specs=(
            P(("dom", "frame"), None, None),
            P(("dom", "query")),
            P(None, ("dom", "query")),
            P(),
            P(),
            P(None, None, "split"),
            P(None, "split", None),
        ),
        out_specs=P(("dom", "query"), "frame", None),
        check_vma=False,
    )
```

```python
import functools
import math

import jax
import jax.numpy as jnp
from jax import lax
from jax.experimental import pallas as pl
from jax.experimental.pallas import tpu as pltpu
from jax.sharding import PartitionSpec as P


LANES = 128
ROOM = 20 * 1024 * 1024
BF16 = jnp.bfloat16
F32 = jnp.float32
VMEM = pl.BlockSpec(memory_space=pltpu.VMEM)
HBM = pl.BlockSpec(memory_space=pltpu.HBM)


def held(value):
    return pltpu.with_memory_space_constraint(value, pltpu.VMEM)


def fixed(value):
    return pltpu.with_memory_space_constraint(value, pltpu.HBM)


def kept(shape, dtype):
    return pltpu.VMEM(shape, dtype)


def call(body, out, count, scratch=(), in_specs=None, out_specs=None, aliases=None):
    many = isinstance(out, tuple)
    if out_specs is None:
        out_specs = (VMEM,) * len(out) if many else VMEM
    return pl.pallas_call(
        body,
        out_shape=out,
        in_specs=[VMEM] * count if in_specs is None else in_specs,
        out_specs=out_specs,
        scratch_shapes=list(scratch),
        input_output_aliases=aliases or {},
        compiler_params=pltpu.CompilerParams(vmem_limit_bytes=ROOM),
    )


def dot(a, b):
    return jnp.dot(a, b, preferred_element_type=F32)


def my_part(whole, part, parts):
    size = whole.shape[-1] // parts
    mine = whole[:, :size]
    for at in range(1, parts):
        mine = jnp.where(part == at, whole[:, at * size : (at + 1) * size], mine)
    return mine


def is_even():
    return lax.rem(lax.axis_index("frame"), 2) == 0


def near_frame():
    return 1 - lax.rem(lax.axis_index("frame"), 2)


def inverse_rms(values, epsilon):
    return lax.rsqrt(jnp.mean(values * values, axis=-1, keepdims=True) + epsilon)


def level_of(stream):
    return (stream * inverse_rms(stream, 1e-5)).astype(BF16).astype(F32)


def pick_body(
    parts,
    frame_hbm,
    pixel_hbm,
    frames_hbm,
    out_ref,
    frames_ref,
    outer_ref,
    frame_ref,
    pixel_ref,
    sems,
):
    frame_count, pixel_count, _ = frames_ref.shape
    loads = [
        pltpu.make_async_copy(frame_hbm, frame_ref, sems.at[0]),
        pltpu.make_async_copy(pixel_hbm, pixel_ref, sems.at[1]),
    ]
    chunk = min(512, pixel_count)
    spots = [(at, t) for at in range(0, pixel_count, chunk) for t in range(frame_count)]
    maps = [
        pltpu.make_async_copy(
            frames_hbm.at[t, pl.ds(at, chunk)], frames_ref.at[t, pl.ds(at, chunk)], sems.at[2 + k]
        )
        for k, (at, t) in enumerate(spots)
    ]
    part = lax.axis_index("split")
    share = outer_ref.shape[0]
    side_of_pair = lax.rem(lax.axis_index("query"), 2)
    outer = pltpu.make_async_copy(
        frames_hbm.at[1 - near_frame(), pl.ds((2 * part + side_of_pair) * share, share)], outer_ref, sems.at[2 + len(maps)]
    )
    for copy in loads + maps + [outer]:
        copy.start()
    for copy in loads:
        copy.wait()
    first = lax.axis_index("frame") * frame_count
    side = math.isqrt(pixel_count)
    pixel = pixel_ref[...]
    local = my_part(frame_ref[...], part, parts) - first
    row = my_part(pixel[0:1], part, parts)
    col = my_part(pixel[1:2], part, parts)
    place = row * side + col
    count = place.shape[1]
    line = lax.broadcasted_iota(jnp.int32, (8, count), 0)
    both = jnp.transpose(jnp.where(line == 0, place, local))
    place = jnp.broadcast_to(both[:, :1], (count, LANES))
    local = jnp.broadcast_to(both[:, 1:2], (count, LANES))
    order = lax.broadcasted_iota(jnp.int32, (count, LANES), 1)
    totals = [None] * frame_count
    for at in range(0, pixel_count, chunk):
        hot = jnp.concatenate(
            [
                jnp.where(place == order + k, 1.0, 0.0).astype(BF16)
                for k in range(at, at + chunk, LANES)
            ],
            axis=1,
        )
        for t in range(frame_count):
            maps[spots.index((at, t))].wait()
        for t in range(frame_count):
            part_sum = dot(hot, frames_ref[t, at : at + chunk, :])
            totals[t] = part_sum if at == 0 else totals[t] + part_sum
    for b in range(0, out_ref.shape[1], LANES):
        picked = jnp.zeros((count, LANES), F32)
        for t in range(frame_count):
            picked = jnp.where(local == t, totals[t][:, b : b + LANES], picked)
        out_ref[:, b : b + LANES] = picked.astype(BF16)
    outer.wait()


def join_body(a_ref, b_ref, out_ref):
    out_ref[...] = a_ref[...] + b_ref[...]


def attend_split(features, blocks, scale, scratch):
    rows, size = features.shape
    sums = [pltpu.ACC(k % 2)((rows, size), F32) for k in range(len(blocks))]
    return pl.run_scoped(functools.partial(attend_units, features, blocks, scale, scratch), *sums)


def attend_units(features, blocks, scale, scratch, *sums):
    score_ref, weight_ref, sum_ref = scratch
    rows, size = features.shape
    step = 32
    for j, block in enumerate(blocks):
        unit, slot = j % 2, j // 2
        at = j * size
        acc = sums[j]
        pltpu.matmul_push_rhs(block[...], slot % 2, unit, transpose=True)
        pltpu.matmul_acc_lhs(acc, features, load_staged_rhs=slot % 2)
        score_ref[0, :, at : at + size] = pltpu.matmul_pop(acc)
    for at in range(0, rows, step):
        scores = score_ref[0, at : at + step, :]
        peak = jnp.max(scores, axis=-1, keepdims=True)
        expd = jnp.exp2((scores - peak) * scale)
        total = jnp.sum(expd, axis=-1, keepdims=True)
        sum_ref[0, at : at + step, :] = jnp.broadcast_to(total, (step, LANES))
        weight_ref[0, at : at + step, :] = expd.astype(BF16)
    for j, block in enumerate(blocks):
        unit, slot = j % 2, j // 2
        at = j * size
        pltpu.matmul_push_rhs(block[...], slot % 2, unit)
        pltpu.matmul_acc_lhs(
            sums[unit], weight_ref[0, :, at : at + size], load_staged_rhs=slot % 2
        )
    pooled = pltpu.matmul_pop(sums[0]) + pltpu.matmul_pop(sums[1])
    total = sum_ref[0, :, :1]
    mean = jnp.mean(pooled * pooled, axis=-1, keepdims=True)
    return (pooled * lax.rsqrt(mean + 1e-6 * total * total)).astype(BF16)


def blocks_of(frames_ref, t):
    size = frames_ref.shape[2]
    return [frames_ref.at[t, pl.ds(at, size)] for at in range(0, frames_ref.shape[1], size)]


def near_body(scale, a_ref, b_ref, frames_ref, features_ref, normed_ref, *scratch):
    features = a_ref[...] + b_ref[...]
    features_ref[...] = features
    normed_ref[...] = attend_split(features, blocks_of(frames_ref, near_frame()), scale, scratch)


def far_body(scale, features_ref, frames_ref, normed_ref, *scratch):
    blocks = blocks_of(frames_ref, 1 - near_frame())
    normed_ref[...] = attend_split(features_ref[...], blocks, scale, scratch)


def has_outer(devices):
    place = lax.axis_index("frame")
    return jnp.where(is_even(), place > 0, place < devices - 1)


def halo_body(devices, scale, features_ref, a_ref, b_ref, c_ref, d_ref, normed_ref, *scratch):
    inside = has_outer(devices)

    @pl.when(inside)
    def _():
        blocks = [a_ref, b_ref, c_ref, d_ref]
        normed_ref[...] = attend_split(features_ref[...], blocks, scale, scratch)

    @pl.when(jnp.logical_not(inside))
    def _():
        normed_ref[...] = jnp.zeros_like(normed_ref)


def taps_of(taps_ref):
    width = taps_ref.shape[1] // 3
    first, middle, last = (taps_ref[:, k * width : (k + 1) * width] for k in range(3))
    even = is_even()
    return jnp.where(even, last, first), middle, jnp.where(even, first, last)


def own_body(features_ref, near_ref, far_ref, in_ref, taps_ref, base_ref, near_out, far_out):
    channels = features_ref.shape[1]
    near_tap, middle, far_tap = taps_of(taps_ref)
    base = dot(features_ref[...], in_ref[channels:, :])
    base_ref[...] = base
    near = dot(near_ref[...], in_ref[:channels, :]) + base
    far = dot(far_ref[...], in_ref[:channels, :]) + base
    near_level, far_level = level_of(near), level_of(far)
    near_out[...] = near + middle * near_level + far_tap * far_level
    far_out[...] = far + middle * far_level + near_tap * near_level


def with_halo(halo_ref, own_ref, base_ref, in_ref, tap, inside):
    channels = halo_ref.shape[1]
    halo = level_of(dot(halo_ref[...], in_ref[:channels, :]) + base_ref[...])
    return own_ref[...] + jnp.where(inside, tap, 0.0) * halo


def mix(stream, ups, downs, hidden_ref):
    gated = (stream * inverse_rms(stream, 1e-5)).astype(BF16)
    base = 0
    total = None
    for up_ref, down_ref in zip(ups, downs):
        units = up_ref.shape[2]
        step = min(256, units)
        for at in range(0, units, step):
            x = dot(gated, up_ref[0, :, at : at + step]).astype(BF16)
            inner = x * (x * x * BF16(0.044715 * math.sqrt(2 / math.pi)) + BF16(math.sqrt(2 / math.pi)))
            hidden_ref[:, base + at : base + at + step] = x + x * jnp.tanh(inner)
        base += units
    base = 0
    for up_ref, down_ref in zip(ups, downs):
        units = up_ref.shape[2]
        part = dot(hidden_ref[:, base : base + units], down_ref[0])
        total = part if total is None else total + part
        base += units
    return stream + 0.5 * total


def mix_far_body(
    devices, halo_ref, own_ref, base_ref, in_ref, taps_ref, up_a, up_b, down_a, down_b, out_ref, hidden_ref
):
    inside = has_outer(devices)
    out_ref[...] = own_ref[...]

    @pl.when(inside)
    def _():
        _, _, tap = taps_of(taps_ref)
        out_ref[...] = with_halo(halo_ref, own_ref, base_ref, in_ref, tap, inside)

    out_ref[...] = mix(out_ref[...], (up_a, up_b), (down_a, down_b), hidden_ref)


def mix_near_body(
    devices,
    halo_ref,
    own_ref,
    base_ref,
    in_ref,
    taps_ref,
    up_a,
    up_b,
    down_a,
    down_b,
    far_ref,
    out_ref,
    hidden_ref,
    line_ref,
):
    place = lax.axis_index("frame")
    even = is_even()
    inside = jnp.logical_not(even) | (place < devices - 1)
    tap, _, _ = taps_of(taps_ref)
    stream = with_halo(halo_ref, own_ref, base_ref, in_ref, tap, inside)
    near = mix(stream, (up_a, up_b), (down_a, down_b), hidden_ref)
    far = far_ref[...]
    rows, width = far.shape
    blocks = width // LANES
    for t, value in ((0, jnp.where(even, far, near)), (1, jnp.where(even, near, far))):
        for b in range(blocks):
            line_ref[pl.ds(b * 2 + t, rows, stride=blocks * 2), :] = value[
                :, b * LANES : (b + 1) * LANES
            ]
    out_ref[...] = line_ref[...].astype(BF16)


def copy_lines(source_ref, target_ref, first, sems):
    rows = source_ref.shape[0]
    count = sems.shape[0]
    size = rows // count
    copies = [
        pltpu.make_async_copy(
            source_ref.at[pl.ds(k * size, size)],
            target_ref.at[pl.ds(first + k * size, size)],
            sems.at[k],
        )
        for k in range(count)
    ]
    for copy in copies:
        copy.start()
    for copy in copies:
        copy.wait()


def place_body(own_ref, out_ref, sems):
    copy_lines(own_ref, out_ref, lax.axis_index("split") * own_ref.shape[0], sems)


def merge_body(other_ref, _, out_ref, sems):
    copy_lines(other_ref, out_ref, (1 - lax.axis_index("split")) * other_ref.shape[0], sems)


def on_device(frames, query_frame, query_pixel, in_weight, conv_weight, up_weight, down_weight):
    frame_count, pixel_count, channels = frames.shape
    query_count = query_frame.shape[0]
    width = in_weight.shape[1]
    units = up_weight.shape[2]
    parts = lax.axis_size("split")
    devices = lax.axis_size("frame")
    assert parts == 2 and frame_count == 2 and devices > 1 and devices & (devices - 1) == 0
    rows = query_count // parts
    swap = [(0, 1), (1, 0)]
    flips = lambda mask: [(i, i ^ mask) for i in range(devices)]
    mine, frames, outer = call(
        functools.partial(pick_body, parts),
        (
            kept((rows, channels), BF16),
            kept(frames.shape, BF16),
            kept((pixel_count // parts // 2, channels), BF16),
        ),
        3,
        scratch=(
            pltpu.VMEM((1, query_count), jnp.int32),
            pltpu.VMEM(query_pixel.shape, jnp.int32),
            pltpu.SemaphoreType.DMA((3 + frame_count * pixel_count // min(512, pixel_count),)),
        ),
        in_specs=[HBM] * 3,
    )(*(fixed(x) for x in (query_frame.reshape(1, query_count), query_pixel, frames)))
    pairs = [
        (parts * i + c, parts * (i + 1) + c) for i in range(1, devices - 1, 2) for c in range(parts)
    ] + [(parts * i, parts * i + 1) for i in (0, devices - 1)]
    masks = [2 * (1 << k) - 1 for k in range(devices.bit_length() - 1)]
    theirs = lax.ppermute(mine, "frame", flips(masks[0]))
    outer = lax.ppermute(outer, ("frame", "split"), pairs + [(b, a) for a, b in pairs])
    up_other = lax.ppermute(up_weight, "split", swap)
    down_other = lax.ppermute(down_weight, "split", swap)
    theirs, up_other, down_other = held(theirs), held(up_other), held(down_other)
    outer = held(outer)
    for mask in masks[1:]:
        mine = call(join_body, kept((rows, channels), BF16), 2)(mine, theirs)
        theirs = lax.ppermute(mine, "frame", flips(mask))
        theirs = held(theirs)
    groups = lax.axis_size("query")
    assert groups % 2 == 0
    outer_b = lax.ppermute(outer, "query", [(g, g ^ 1) for g in range(groups)])
    outer_b = held(outer_b)
    outer_c = lax.ppermute(outer, "split", swap)
    outer_d = lax.ppermute(outer_b, "split", swap)
    outers = (outer, outer_b, held(outer_c), held(outer_d))
    in_weight = held(in_weight)
    taps = held(conv_weight.reshape(1, conv_weight.shape[1] * width))
    weights = (held(up_weight), up_other, held(down_weight), down_other)
    scale = math.log2(math.e) / math.sqrt(channels)
    attention = lambda count: (
        pltpu.VMEM((count, rows, pixel_count), F32),
        pltpu.VMEM((count, rows, pixel_count), BF16),
        pltpu.VMEM((count, rows, LANES), F32),
    )
    small = kept((rows, channels), BF16)
    wide = kept((rows, width), F32)
    features, near = call(
        functools.partial(near_body, scale), (small, small), 3, attention(1)
    )(mine, theirs, frames)
    near_halo = lax.ppermute(near, "frame", flips(1))
    near_halo = held(near_halo)
    far = call(functools.partial(far_body, scale), small, 2, attention(1))(features, frames)
    base, own_near, own_far = call(own_body, (wide,) * 3, 5)(features, near, far, in_weight, taps)
    far_halo = call(functools.partial(halo_body, devices, scale), small, 5, attention(1))(
        features, *outers
    )
    hidden = pltpu.VMEM((rows, parts * units), BF16)
    far = call(functools.partial(mix_far_body, devices), wide, 9, (hidden,))(
        far_halo, own_far, base, in_weight, taps, *weights
    )
    blocks = width // LANES
    lines = rows * blocks * frame_count
    own = call(
        functools.partial(mix_near_body, devices),
        kept((lines, LANES), BF16),
        10,
        (hidden, pltpu.VMEM((lines, LANES), F32)),
    )(near_halo, own_near, base, in_weight, taps, *weights, far)
    other = held(lax.ppermute(own, "split", swap))
    whole = jax.ShapeDtypeStruct((parts * lines, LANES), BF16)
    moves = (pltpu.SemaphoreType.DMA((4,)),)
    both = call(place_body, whole, 1, moves, out_specs=HBM)(own)
    both = call(
        merge_body, whole, 2, moves, in_specs=[VMEM, HBM], out_specs=HBM, aliases={1: 0}
    )(other, both)
    both = both.reshape(query_count, blocks, frame_count, LANES)
    return both.transpose(0, 2, 1, 3).reshape(query_count, frame_count, width)


def solution(mesh):
    return jax.shard_map(
        on_device,
        mesh=mesh,
        in_specs=(
            P(("dom", "frame"), None, None),
            P(("dom", "query")),
            P(None, ("dom", "query")),
            P(),
            P(),
            P(None, None, "split"),
            P(None, "split", None),
        ),
        out_specs=P(("dom", "query"), "frame", None),
        check_vma=False,
    )
```

```python
import functools
import math

import jax
import jax.numpy as jnp
from jax import lax
from jax.experimental import pallas as pl
from jax.experimental.pallas import tpu as pltpu
from jax.sharding import PartitionSpec as P


LANES = 128
ROOM = 20 * 1024 * 1024
BF16 = jnp.bfloat16
F32 = jnp.float32
VMEM = pl.BlockSpec(memory_space=pltpu.VMEM)
HBM = pl.BlockSpec(memory_space=pltpu.HBM)


def held(value):
    return pltpu.with_memory_space_constraint(value, pltpu.VMEM)


def fixed(value):
    return pltpu.with_memory_space_constraint(value, pltpu.HBM)


def kept(shape, dtype):
    return pltpu.VMEM(shape, dtype)


def call(body, out, count, scratch=(), in_specs=None, out_specs=None, aliases=None):
    many = isinstance(out, tuple)
    if out_specs is None:
        out_specs = (VMEM,) * len(out) if many else VMEM
    return pl.pallas_call(
        body,
        out_shape=out,
        in_specs=[VMEM] * count if in_specs is None else in_specs,
        out_specs=out_specs,
        scratch_shapes=list(scratch),
        input_output_aliases=aliases or {},
        compiler_params=pltpu.CompilerParams(vmem_limit_bytes=ROOM),
    )


def dot(a, b):
    return jnp.dot(a, b, preferred_element_type=F32)


def my_part(whole, part, parts):
    size = whole.shape[-1] // parts
    mine = whole[:, :size]
    for at in range(1, parts):
        mine = jnp.where(part == at, whole[:, at * size : (at + 1) * size], mine)
    return mine


def is_even():
    return lax.rem(lax.axis_index("frame"), 2) == 0


def near_frame():
    return 1 - lax.rem(lax.axis_index("frame"), 2)


def inverse_rms(values, epsilon):
    return lax.rsqrt(jnp.mean(values * values, axis=-1, keepdims=True) + epsilon)


def level_of(stream):
    return (stream * inverse_rms(stream, 1e-5)).astype(BF16).astype(F32)


def pick_body(
    parts,
    frame_hbm,
    pixel_hbm,
    frames_hbm,
    out_ref,
    frames_ref,
    outer_ref,
    frame_ref,
    pixel_ref,
    sems,
):
    frame_count, pixel_count, _ = frames_ref.shape
    loads = [
        pltpu.make_async_copy(frame_hbm, frame_ref, sems.at[0]),
        pltpu.make_async_copy(pixel_hbm, pixel_ref, sems.at[1]),
    ]
    chunk = min(512, pixel_count)
    spots = [(at, t) for at in range(0, pixel_count, chunk) for t in range(frame_count)]
    maps = [
        pltpu.make_async_copy(
            frames_hbm.at[t, pl.ds(at, chunk)], frames_ref.at[t, pl.ds(at, chunk)], sems.at[2 + k]
        )
        for k, (at, t) in enumerate(spots)
    ]
    part = lax.axis_index("split")
    share = outer_ref.shape[0]
    side_of_pair = lax.rem(lax.axis_index("query"), 2)
    outer = pltpu.make_async_copy(
        frames_hbm.at[1 - near_frame(), pl.ds((2 * part + side_of_pair) * share, share)], outer_ref, sems.at[2 + len(maps)]
    )
    for copy in loads + maps + [outer]:
        copy.start()
    for copy in loads:
        copy.wait()
    first = lax.axis_index("frame") * frame_count
    side = math.isqrt(pixel_count)
    pixel = pixel_ref[...]
    local = my_part(frame_ref[...], part, parts) - first
    row = my_part(pixel[0:1], part, parts)
    col = my_part(pixel[1:2], part, parts)
    place = row * side + col
    count = place.shape[1]
    line = lax.broadcasted_iota(jnp.int32, (8, count), 0)
    both = jnp.transpose(jnp.where(line == 0, place, local))
    place = jnp.broadcast_to(both[:, :1], (count, LANES))
    local = jnp.broadcast_to(both[:, 1:2], (count, LANES))
    order = lax.broadcasted_iota(jnp.int32, (count, LANES), 1)
    totals = [None] * frame_count
    for at in range(0, pixel_count, chunk):
        hot = jnp.concatenate(
            [
                jnp.where(place == order + k, 1.0, 0.0).astype(BF16)
                for k in range(at, at + chunk, LANES)
            ],
            axis=1,
        )
        for t in range(frame_count):
            maps[spots.index((at, t))].wait()
        for t in range(frame_count):
            part_sum = dot(hot, frames_ref[t, at : at + chunk, :])
            totals[t] = part_sum if at == 0 else totals[t] + part_sum
    for b in range(0, out_ref.shape[1], LANES):
        picked = jnp.zeros((count, LANES), F32)
        for t in range(frame_count):
            picked = jnp.where(local == t, totals[t][:, b : b + LANES], picked)
        out_ref[:, b : b + LANES] = picked.astype(BF16)
    outer.wait()


def join_body(a_ref, b_ref, out_ref):
    out_ref[...] = a_ref[...] + b_ref[...]


def attend_split(features, blocks, scale, scratch):
    rows, size = features.shape
    sums = [pltpu.ACC(k % 2)((rows, size), F32) for k in range(len(blocks))]
    return pl.run_scoped(functools.partial(attend_units, features, blocks, scale, scratch), *sums)


def attend_units(features, blocks, scale, scratch, *sums):
    score_ref, weight_ref, sum_ref = scratch
    rows, size = features.shape
    step = 32
    for j, block in enumerate(blocks):
        unit, slot = j % 2, j // 2
        at = j * size
        acc = sums[j]
        pltpu.matmul_push_rhs(block[...], slot % 2, unit, transpose=True)
        pltpu.matmul_acc_lhs(acc, features, load_staged_rhs=slot % 2)
        score_ref[0, :, at : at + size] = pltpu.matmul_pop(acc)
    for at in range(0, rows, step):
        scores = score_ref[0, at : at + step, :]
        peak = jnp.max(scores, axis=-1, keepdims=True)
        expd = jnp.exp2((scores - peak) * scale)
        total = jnp.sum(expd, axis=-1, keepdims=True)
        sum_ref[0, at : at + step, :] = jnp.broadcast_to(total, (step, LANES))
        weight_ref[0, at : at + step, :] = expd.astype(BF16)
    for j, block in enumerate(blocks):
        unit, slot = j % 2, j // 2
        at = j * size
        pltpu.matmul_push_rhs(block[...], slot % 2, unit)
        pltpu.matmul_acc_lhs(
            sums[unit], weight_ref[0, :, at : at + size], load_staged_rhs=slot % 2
        )
    pooled = pltpu.matmul_pop(sums[0]) + pltpu.matmul_pop(sums[1])
    total = sum_ref[0, :, :1]
    mean = jnp.mean(pooled * pooled, axis=-1, keepdims=True)
    return (pooled * lax.rsqrt(mean + 1e-6 * total * total)).astype(BF16)


def blocks_of(frames_ref, t):
    size = frames_ref.shape[2]
    return [frames_ref.at[t, pl.ds(at, size)] for at in range(0, frames_ref.shape[1], size)]


def near_body(scale, a_ref, b_ref, frames_ref, features_ref, normed_ref, *scratch):
    features = a_ref[...] + b_ref[...]
    features_ref[...] = features
    normed_ref[...] = attend_split(features, blocks_of(frames_ref, near_frame()), scale, scratch)


def far_body(scale, features_ref, frames_ref, normed_ref, *scratch):
    blocks = blocks_of(frames_ref, 1 - near_frame())
    normed_ref[...] = attend_split(features_ref[...], blocks, scale, scratch)


def has_outer(devices):
    place = lax.axis_index("frame")
    return jnp.where(is_even(), place > 0, place < devices - 1)


def halo_body(devices, scale, features_ref, a_ref, b_ref, c_ref, d_ref, normed_ref, *scratch):
    inside = has_outer(devices)

    @pl.when(inside)
    def _():
        blocks = [a_ref, b_ref, c_ref, d_ref]
        normed_ref[...] = attend_split(features_ref[...], blocks, scale, scratch)

    @pl.when(jnp.logical_not(inside))
    def _():
        normed_ref[...] = jnp.zeros_like(normed_ref)


def taps_of(taps_ref):
    width = taps_ref.shape[1] // 3
    first, middle, last = (taps_ref[:, k * width : (k + 1) * width] for k in range(3))
    even = is_even()
    return jnp.where(even, last, first), middle, jnp.where(even, first, last)


def own_body(features_ref, near_ref, far_ref, in_ref, taps_ref, base_ref, near_out, far_out):
    channels = features_ref.shape[1]
    near_tap, middle, far_tap = taps_of(taps_ref)
    base = dot(features_ref[...], in_ref[channels:, :])
    base_ref[...] = base
    near = dot(near_ref[...], in_ref[:channels, :]) + base
    far = dot(far_ref[...], in_ref[:channels, :]) + base
    near_level, far_level = level_of(near), level_of(far)
    near_out[...] = near + middle * near_level + far_tap * far_level
    far_out[...] = far + middle * far_level + near_tap * near_level


def with_halo(halo_ref, own_ref, base_ref, in_ref, tap, inside):
    channels = halo_ref.shape[1]
    halo = level_of(dot(halo_ref[...], in_ref[:channels, :]) + base_ref[...])
    return own_ref[...] + jnp.where(inside, tap, 0.0) * halo


def mix(stream, ups, downs, hidden_ref):
    gated = (stream * inverse_rms(stream, 1e-5)).astype(BF16)
    base = 0
    total = None
    for up_ref, down_ref in zip(ups, downs):
        units = up_ref.shape[2]
        step = min(512, units)
        for at in range(0, units, step):
            x = dot(gated, up_ref[0, :, at : at + step]).astype(BF16)
            inner = x * (x * x * BF16(0.044715 * math.sqrt(2 / math.pi)) + BF16(math.sqrt(2 / math.pi)))
            hidden_ref[:, base + at : base + at + step] = x + x * jnp.tanh(inner)
        part = dot(hidden_ref[:, base : base + units], down_ref[0])
        total = part if total is None else total + part
        base += units
    return stream + 0.5 * total


def mix_far_body(
    devices, halo_ref, own_ref, base_ref, in_ref, taps_ref, up_a, up_b, down_a, down_b, out_ref, hidden_ref
):
    inside = has_outer(devices)
    out_ref[...] = own_ref[...]

    @pl.when(inside)
    def _():
        _, _, tap = taps_of(taps_ref)
        out_ref[...] = with_halo(halo_ref, own_ref, base_ref, in_ref, tap, inside)

    out_ref[...] = mix(out_ref[...], (up_a, up_b), (down_a, down_b), hidden_ref)


def mix_near_body(
    devices,
    halo_ref,
    own_ref,
    base_ref,
    in_ref,
    taps_ref,
    up_a,
    up_b,
    down_a,
    down_b,
    far_ref,
    out_ref,
    hidden_ref,
    line_ref,
):
    place = lax.axis_index("frame")
    even = is_even()
    inside = jnp.logical_not(even) | (place < devices - 1)
    tap, _, _ = taps_of(taps_ref)
    stream = with_halo(halo_ref, own_ref, base_ref, in_ref, tap, inside)
    near = mix(stream, (up_a, up_b), (down_a, down_b), hidden_ref)
    far = far_ref[...]
    rows, width = far.shape
    blocks = width // LANES
    for t, value in ((0, jnp.where(even, far, near)), (1, jnp.where(even, near, far))):
        for b in range(blocks):
            line_ref[pl.ds(b * 2 + t, rows, stride=blocks * 2), :] = value[
                :, b * LANES : (b + 1) * LANES
            ]
    out_ref[...] = line_ref[...].astype(BF16)


def copy_lines(source_ref, target_ref, first, sems):
    rows = source_ref.shape[0]
    count = sems.shape[0]
    size = rows // count
    copies = [
        pltpu.make_async_copy(
            source_ref.at[pl.ds(k * size, size)],
            target_ref.at[pl.ds(first + k * size, size)],
            sems.at[k],
        )
        for k in range(count)
    ]
    for copy in copies:
        copy.start()
    for copy in copies:
        copy.wait()


def place_body(own_ref, out_ref, sems):
    copy_lines(own_ref, out_ref, lax.axis_index("split") * own_ref.shape[0], sems)


def merge_body(other_ref, _, out_ref, sems):
    copy_lines(other_ref, out_ref, (1 - lax.axis_index("split")) * other_ref.shape[0], sems)


def on_device(frames, query_frame, query_pixel, in_weight, conv_weight, up_weight, down_weight):
    frame_count, pixel_count, channels = frames.shape
    query_count = query_frame.shape[0]
    width = in_weight.shape[1]
    units = up_weight.shape[2]
    parts = lax.axis_size("split")
    devices = lax.axis_size("frame")
    assert parts == 2 and frame_count == 2 and devices > 1 and devices & (devices - 1) == 0
    rows = query_count // parts
    swap = [(0, 1), (1, 0)]
    flips = lambda mask: [(i, i ^ mask) for i in range(devices)]
    mine, frames, outer = call(
        functools.partial(pick_body, parts),
        (
            kept((rows, channels), BF16),
            kept(frames.shape, BF16),
            kept((pixel_count // parts // 2, channels), BF16),
        ),
        3,
        scratch=(
            pltpu.VMEM((1, query_count), jnp.int32),
            pltpu.VMEM(query_pixel.shape, jnp.int32),
            pltpu.SemaphoreType.DMA((3 + frame_count * pixel_count // min(512, pixel_count),)),
        ),
        in_specs=[HBM] * 3,
    )(*(fixed(x) for x in (query_frame.reshape(1, query_count), query_pixel, frames)))
    pairs = [
        (parts * i + c, parts * (i + 1) + c) for i in range(1, devices - 1, 2) for c in range(parts)
    ] + [(parts * i, parts * i + 1) for i in (0, devices - 1)]
    masks = [2 * (1 << k) - 1 for k in range(devices.bit_length() - 1)]
    theirs = lax.ppermute(mine, "frame", flips(masks[0]))
    outer = lax.ppermute(outer, ("frame", "split"), pairs + [(b, a) for a, b in pairs])
    up_other = lax.ppermute(up_weight, "split", swap)
    down_other = lax.ppermute(down_weight, "split", swap)
    theirs, up_other, down_other = held(theirs), held(up_other), held(down_other)
    outer = held(outer)
    for mask in masks[1:]:
        mine = call(join_body, kept((rows, channels), BF16), 2)(mine, theirs)
        theirs = lax.ppermute(mine, "frame", flips(mask))
        theirs = held(theirs)
    groups = lax.axis_size("query")
    assert groups % 2 == 0
    outer_b = lax.ppermute(outer, "query", [(g, g ^ 1) for g in range(groups)])
    outer_b = held(outer_b)
    outer_c = lax.ppermute(outer, "split", swap)
    outer_d = lax.ppermute(outer_b, "split", swap)
    outers = (outer, outer_b, held(outer_c), held(outer_d))
    in_weight = held(in_weight)
    taps = held(conv_weight.reshape(1, conv_weight.shape[1] * width))
    weights = (held(up_weight), up_other, held(down_weight), down_other)
    scale = math.log2(math.e) / math.sqrt(channels)
    attention = lambda count: (
        pltpu.VMEM((count, rows, pixel_count), F32),
        pltpu.VMEM((count, rows, pixel_count), BF16),
        pltpu.VMEM((count, rows, LANES), F32),
    )
    small = kept((rows, channels), BF16)
    wide = kept((rows, width), F32)
    features, near = call(
        functools.partial(near_body, scale), (small, small), 3, attention(1)
    )(mine, theirs, frames)
    near_halo = lax.ppermute(near, "frame", flips(1))
    near_halo = held(near_halo)
    far = call(functools.partial(far_body, scale), small, 2, attention(1))(features, frames)
    base, own_near, own_far = call(own_body, (wide,) * 3, 5)(features, near, far, in_weight, taps)
    far_halo = call(functools.partial(halo_body, devices, scale), small, 5, attention(1))(
        features, *outers
    )
    hidden = pltpu.VMEM((rows, parts * units), BF16)
    far = call(functools.partial(mix_far_body, devices), wide, 9, (hidden,))(
        far_halo, own_far, base, in_weight, taps, *weights
    )
    blocks = width // LANES
    lines = rows * blocks * frame_count
    own = call(
        functools.partial(mix_near_body, devices),
        kept((lines, LANES), BF16),
        10,
        (hidden, pltpu.VMEM((lines, LANES), F32)),
    )(near_halo, own_near, base, in_weight, taps, *weights, far)
    other = held(lax.ppermute(own, "split", swap))
    whole = jax.ShapeDtypeStruct((parts * lines, LANES), BF16)
    moves = (pltpu.SemaphoreType.DMA((4,)),)
    both = call(place_body, whole, 1, moves, out_specs=HBM)(own)
    both = call(
        merge_body, whole, 2, moves, in_specs=[VMEM, HBM], out_specs=HBM, aliases={1: 0}
    )(other, both)
    both = both.reshape(query_count, blocks, frame_count, LANES)
    return both.transpose(0, 2, 1, 3).reshape(query_count, frame_count, width)


def solution(mesh):
    return jax.shard_map(
        on_device,
        mesh=mesh,
        in_specs=(
            P(("dom", "frame"), None, None),
            P(("dom", "query")),
            P(None, ("dom", "query")),
            P(),
            P(),
            P(None, None, "split"),
            P(None, "split", None),
        ),
        out_specs=P(("dom", "query"), "frame", None),
        check_vma=False,
    )
```
